256 devices in a mesh: row: 16 (over y_hi, x, core), col: 16 (over z, y_lo).
Axes of the slice: x: 4, y: 4 (y_hi: 2, y_lo: 2; y = y_hi * 2 + y_lo), z: 8, core: 2. Of those that a mesh axis runs over, the one named last changes fastest.
Arguments:
- slab: bfloat16 [2, 640, 640, 640], P(None, 'col', 'row'), may hold values from -6 to 6
- coef_virtual: bfloat16 [640, 576], replicated, may hold values from -0.25 to 0.25
- coef_occupied: bfloat16 [640, 64], replicated, may hold values from -0.25 to 0.25
- occ_level: int32 [64], replicated, may hold values from -160 to -16
- virt_level: int32 [576], replicated, may hold values from 16 to 192
- orbital_index: int32 [2], replicated, may hold values from 0 to 63
Outputs:
- back_slab: bfloat16 [2, 640, 640, 640], P(None, 'col', 'row')
The draws below stay inside these ranges and needn't reach their ends.
All inputs are finite; a program needn't handle non-finite values.
Results may differ from the reference program's by a relative error of at most 0.008.
Values may be sent and summed in bfloat16 or wider, within the bound.
No kernel may reach another device: no remote copies, remote signals or barrier semaphores. Data moves between devices by JAX's collectives and lax.ppermute only.
A program may use at most 64 MiB of HBM per device.

```python
import jax
import jax.numpy as jnp

NB = 640
NO = 64
NV = 576
NI = 2


def place_ends(values, stream_key, least, largest):
    longest = values.shape.index(max(values.shape))
    spots = []
    for shift in (0, 1):
        where = [jax.random.randint(jax.random.fold_in(stream_key, axis), (), 0, length) for axis, length in enumerate(values.shape)]
        where[longest] = (where[longest] + shift) % values.shape[longest]
        spots.append(tuple(where))
    return values.at[spots[0]].set(least).at[spots[1]].set(largest)


def block_scale(key, shape, cuts, least, high):
    loudness = 1.0
    for dim, blocks in cuts:
        draws = jax.random.uniform(jax.random.fold_in(jax.random.fold_in(key, 6), dim), (blocks,), jnp.float32, least / len(cuts), high / len(cuts))
        loudness = loudness * jnp.repeat(jnp.exp(draws), shape[dim] // blocks).reshape((-1,) + (1,) * (len(shape) - 1 - dim))
    return loudness


def normal_values(own_key, dims, deviation, reach, cuts=(), kind=jnp.bfloat16):
    drawn = jax.random.normal(own_key, dims, jnp.float32) * deviation
    if len(cuts) > 0:
        drawn = block_scale(own_key, dims, cuts, -0.22, 0.18) * drawn
    return jnp.clip(drawn, min=-reach, max=reach).astype(kind)


def setup_inputs(seed: int = 0) -> dict:
    key_of = jax.random.split(jax.random.key(seed), 7)
    return {
        "slab": normal_values(key_of[0], (NI, NB, NB, NB), 1.0, 6.0, ((1, 16), (2, 16))),
        "coef_virtual": normal_values(key_of[1], (NB, NV), NB ** -0.5, 0.25),
        "coef_occupied": normal_values(key_of[2], (NB, NO), NB ** -0.5, 0.25),
        "occ_level": place_ends(jax.random.randint(key_of[3], (NO,), -160, -15), jax.random.fold_in(key_of[3], 1), -160, (-15) - 1).astype(jnp.int32),
        "virt_level": place_ends(jax.random.randint(key_of[4], (NV,), 16, 193), jax.random.fold_in(key_of[4], 1), 16, 192).astype(jnp.int32),
        "orbital_index": jax.random.randint(key_of[5], (NI,), 0, NO).astype(jnp.int32),
    }


def one_orbital(block, energy_i, coef_virtual, coef_occupied, eo, ev):
    first = jnp.dot(block.reshape(NB * NB, NB), coef_virtual, preferred_element_type=jnp.float32)
    first = first.astype(jnp.bfloat16).reshape(NB, NB * NV)
    second = jnp.dot(first.T, coef_occupied, preferred_element_type=jnp.float32).astype(jnp.bfloat16)
    third = jnp.dot(coef_virtual.T, second.reshape(NB, NV * NO), preferred_element_type=jnp.float32)
    third = third.reshape(NV, NV, NO)
    denom = ev[:, None, None] + ev[None, :, None] - energy_i - eo[None, None, :]
    amplitude = (third / denom).astype(jnp.bfloat16)
    back_one = jnp.dot(coef_virtual, amplitude.reshape(NV, NV * NO), preferred_element_type=jnp.float32)
    back_one = back_one.astype(jnp.bfloat16).reshape(NB * NV, NO)
    back_two = jnp.dot(back_one, coef_occupied.T, preferred_element_type=jnp.float32).astype(jnp.bfloat16)
    back_two = jnp.transpose(back_two.reshape(NB, NV, NB), (2, 0, 1)).reshape(NB * NB, NV)
    result = jnp.dot(back_two, coef_virtual.T, preferred_element_type=jnp.float32).astype(jnp.bfloat16)
    return result.reshape(NB, NB, NB)


def reference(slab, coef_virtual, coef_occupied, occ_level, virt_level, orbital_index):
    eo = occ_level.astype(jnp.float32) / 64.0
    ev = virt_level.astype(jnp.float32) / 64.0
    picks = orbital_index[:, None] == jnp.arange(NO, dtype=jnp.int32)[None, :]
    energy_i = jnp.sum(jnp.where(picks, eo[None, :], jnp.float32(0.0)), axis=1)
    outputs = []
    for orbit in range(NI):
        outputs.append(one_orbital(slab[orbit], energy_i[orbit], coef_virtual, coef_occupied, eo, ev))
    return jnp.stack(outputs, axis=0)
```

```python
import jax
import jax.numpy as jnp
from jax import lax
from jax.sharding import Mesh, PartitionSpec as P

NB = 640
NO = 64
NV = 576
NROW = 16
NZ = 8
TILE = 8
JB = NO // NZ
LB = NB // 16
MB = NB // NROW
HALF = NV // 2
BF = jnp.bfloat16
F32 = jnp.float32
CW = [(i, (i + 1) % NZ) for i in range(NZ)]
CCW = [(i, (i - 1) % NZ) for i in range(NZ)]
SWAP = [(0, 1), (1, 0)]
STREAMS = (((0, 1, 2), 4, 3), ((3, 4), 3, 4))


def dot(a, b):
    return lax.dot_general(a, b, (((1,), (0,)), ((), ())), preferred_element_type=F32)


def spread(coef_t, base, zi):
    rows, cols = NO * TILE, LB * TILE
    lam = lax.broadcasted_iota(jnp.int32, (NB, cols), 0)
    col = lax.broadcasted_iota(jnp.int32, (NB, cols), 1)
    pick = (lam == base + col // TILE).astype(BF)
    wide = dot(coef_t, pick).astype(BF)
    row = lax.broadcasted_iota(jnp.int32, (rows, NO), 0)
    occ = lax.broadcasted_iota(jnp.int32, (rows, NO), 1)
    block = row // TILE
    want = ((zi + block // JB) % NZ) * JB + block % JB
    tall = dot((occ == want).astype(BF), wide)
    row = lax.broadcasted_iota(jnp.int32, (rows, cols), 0)
    col = lax.broadcasted_iota(jnp.int32, (rows, cols), 1)
    return jnp.where(row % TILE == col % TILE, tall, 0.0).astype(BF)


def add(*terms):
    total = terms[0].astype(F32)
    for term in terms[1:]:
        total = total + term.astype(F32)
    return total.astype(BF)


def reduce_ring(parts, ahead, behind):
    up = parts[ahead]
    for k in range(ahead - 1, -1, -1):
        up = lax.ppermute(up, "z", CW)
        if k:
            up = add(up, parts[k])
    down = parts[NZ - behind]
    for k in range(behind - 1, -1, -1):
        down = lax.ppermute(down, "z", CCW)
        if k:
            down = add(down, parts[NZ - k])
    return add(parts[0], up, down)


def gather_ring(own, ahead, behind):
    slots = [own] + [None] * (NZ - 1)
    held = own
    for k in range(1, ahead + 1):
        held = lax.ppermute(held, "z", CW)
        slots[NZ - k] = held
    held = own
    for k in range(1, behind + 1):
        held = lax.ppermute(held, "z", CCW)
        slots[k] = held
    return slots


def local(slab, coef_virtual, coef_occupied, occ_level, virt_level, orbital_index):
    zi = lax.axis_index("z")
    yi = lax.axis_index("ylo")
    ri = lax.axis_index("row")
    eo = occ_level.astype(F32) / 64.0
    ev = virt_level.astype(F32) / 64.0
    occs = jnp.arange(NO, dtype=jnp.int32)
    chosen = jnp.sum(jnp.where(jnp.arange(2) == yi, orbital_index, 0))
    energy_i = jnp.sum(jnp.where(occs == chosen, eo, 0.0))
    energy_j = jnp.sum(jnp.where(occs == zi * JB + ri % JB, eo, 0.0))
    halves = (coef_virtual[:, :HALF], coef_virtual[:, HALF:])
    ev_half = jnp.where(ri // JB == 0, ev[:HALF], ev[HALF:])
    denom = ev[:, None] + ev_half[None, :] - energy_i - energy_j

    mine = lax.dynamic_index_in_dim(slab, yi, 0, keepdims=False)
    other = lax.dynamic_index_in_dim(slab, 1 - yi, 0, keepdims=False)
    coef_t = coef_occupied.T
    k_mine = spread(coef_t, zi * 2 * LB + yi * LB, zi)
    k_other = spread(coef_t, zi * 2 * LB + (1 - yi) * LB, zi)

    pieces = []
    for tiles, ahead, behind in STREAMS:
        lo, hi = tiles[0] * TILE, (tiles[-1] + 1) * TILE
        swapped = lax.ppermute(other[:, lo:hi], "ylo", SWAP)
        partial = []
        for t in tiles:
            here = mine[:, t * TILE : (t + 1) * TILE].reshape(LB * TILE, NB)
            came = swapped[:, t * TILE - lo : (t + 1) * TILE - lo].reshape(LB * TILE, NB)
            whole = dot(k_mine, here) + dot(k_other, came)
            partial.append(whole.astype(BF).reshape(NZ, JB, TILE, NB))
        parts = [jnp.concatenate([p[k] for p in partial], axis=1) for k in range(NZ)]
        summed = reduce_ring(parts, ahead, behind)
        flat = summed.reshape(JB * (hi - lo), NB)
        pieces.append([dot(flat, h).astype(BF).reshape(JB, hi - lo, HALF) for h in halves])
    first = jnp.concatenate(
        [jnp.concatenate([p[h] for p in pieces], axis=1) for h in range(2)], axis=0
    )
    second = lax.all_to_all(first, "row", 0, 0, tiled=True).reshape(NB, HALF)
    third = dot(coef_virtual.T, second)
    amplitude = (third / denom).astype(BF)
    back_one = dot(coef_virtual, amplitude).astype(BF).reshape(NROW, MB, HALF)
    back = lax.all_to_all(back_one, "row", 0, 0, tiled=True)
    back = back.reshape(2, JB * MB, HALF)
    wide = dot(back[0], halves[0].T) + dot(back[1], halves[1].T)
    wide = wide.astype(BF).reshape(JB, MB, NB)

    kept, got = [], []
    for tiles, ahead, behind in STREAMS:
        lo, hi = tiles[0] * TILE, (tiles[-1] + 1) * TILE
        slots = gather_ring(wide[:, lo:hi], ahead, behind)
        send = []
        for t in tiles:
            stack = jnp.concatenate([s[:, t * TILE - lo : (t + 1) * TILE - lo] for s in slots], axis=0)
            stack = stack.reshape(NO * TILE, NB)
            send.append(dot(k_other.T, stack).astype(BF).reshape(LB, TILE, NB))
            kept.append(dot(k_mine.T, stack).astype(BF).reshape(LB, TILE, NB))
        got.append(lax.ppermute(jnp.concatenate(send, axis=1), "ylo", SWAP))
    kept = jnp.concatenate(kept, axis=1)
    got = jnp.concatenate(got, axis=1)
    return jnp.stack([jnp.where(yi == 0, kept, got), jnp.where(yi == 0, got, kept)], axis=0)


def solution(mesh):
    fine = Mesh(mesh.devices.reshape(NROW, NZ, 2), ("row", "z", "ylo"))
    slab = P(None, ("z", "ylo"), "row", None)
    return jax.shard_map(
        local, mesh=fine, in_specs=(slab, P(), P(), P(), P(), P()), out_specs=slab, check_vma=False
    )
```

```python
import jax
import jax.numpy as jnp
from jax import lax
from jax.experimental import pallas as pl
from jax.experimental.pallas import tpu as pltpu
from jax.sharding import Mesh, PartitionSpec as P


NB = 640
NO = 64
NV = 576
NROW = 16
NZ = 8
TILE = 8
JB = NO // NZ
LB = NB // 16
MB = NB // NROW
HALF = NV // 2
RW = NO * TILE
CL = LB * TILE
BF = jnp.bfloat16
F32 = jnp.float32
SWAP = [(0, 1), (1, 0)]
YT, ZT = 3, 2
YM, ZM = YT * TILE, ZT * TILE


def dot(a, b):
    return lax.dot_general(a, b, (((1,), (0,)), ((), ())), preferred_element_type=F32)


def call(body, grid, in_specs, out_specs, out_shape, args, scalars=None, aliases=None, flops=0):
    nbytes = sum(a.size * a.dtype.itemsize for a in args) // 2
    spec = pltpu.PrefetchScalarGridSpec(
        num_scalar_prefetch=0 if scalars is None else 1,
        grid=grid,
        in_specs=in_specs,
        out_specs=out_specs,
    )
    lead = () if scalars is None else (scalars,)
    return pl.pallas_call(
        body,
        grid_spec=spec,
        out_shape=out_shape,
        input_output_aliases=aliases or {},
        cost_estimate=pl.CostEstimate(flops=flops, bytes_accessed=nbytes, transcendentals=0),
        compiler_params=pltpu.CompilerParams(vmem_limit_bytes=24 * 1024 * 1024),
    )(*lead, *args)


def spread(coef_t, base, zi):
    lam = lax.broadcasted_iota(jnp.int32, (NB, CL), 0)
    col = lax.broadcasted_iota(jnp.int32, (NB, CL), 1)
    pick = (lam == base + col // TILE).astype(BF)
    wide = dot(coef_t, pick).astype(BF)
    row = lax.broadcasted_iota(jnp.int32, (RW, NO), 0)
    occ = lax.broadcasted_iota(jnp.int32, (RW, NO), 1)
    block = row // TILE
    want = ((zi + block // JB) % NZ) * JB + block % JB
    tall = dot((occ == want).astype(BF), wide)
    row = lax.broadcasted_iota(jnp.int32, (RW, CL), 0)
    col = lax.broadcasted_iota(jnp.int32, (RW, CL), 1)
    return jnp.where(row % TILE == col % TILE, tall, 0.0).astype(BF)


def fold(x):
    return x.astype(F32).reshape(x.shape[0] * x.shape[1], x.shape[2]).astype(BF)


def whole(shape):
    return pl.BlockSpec(shape, lambda *_: (0,) * len(shape))


def lift(slab, pick):
    step = 8

    def body(_, src, dst):
        dst[...] = src[0]

    return call(
        body,
        (LB // step,),
        [pl.BlockSpec((1, step, YM, NB), lambda i, s: (s[1], i, 0, 0))],
        pl.BlockSpec((step, YM, NB), lambda i, s: (i, 0, 0)),
        jax.ShapeDtypeStruct((LB, YM, NB), BF),
        (slab,),
        pick,
    )


def y_parts(slab, swapped, k_mine, k_other, pick, first, tiles):
    def body(_, here, came, km, ko, *outs):
        part = dot(km[...], fold(here[0])) + dot(ko[...], fold(came[...]))
        part = part.reshape(NZ, JB, TILE, NB)
        for k in range(NZ):
            outs[k][...] = part[k].astype(BF)

    return call(
        body,
        (tiles,),
        [
            pl.BlockSpec((1, LB, TILE, NB), lambda t, s: (s[0], 0, first + t, 0)),
            pl.BlockSpec((LB, TILE, NB), lambda t, s: (0, t, 0)),
            whole((RW, CL)),
            whole((RW, CL)),
        ],
        [pl.BlockSpec((JB, TILE, NB), lambda t, s: (0, t, 0))] * NZ,
        [jax.ShapeDtypeStruct((JB, tiles * TILE, NB), BF)] * NZ,
        (slab, swapped, k_mine, k_other),
        pick,
        flops=4 * tiles * RW * CL * NB,
    )


def z_parts(slab, k_mine, pick, first, tiles):
    def body(_, here, km, *outs):
        part = dot(km[...], fold(here[0])).reshape(NZ, JB, TILE, NB)
        for k in range(NZ):
            outs[k][0] = part[k].astype(BF)

    return call(
        body,
        (2, tiles),
        [
            pl.BlockSpec((1, LB, TILE, NB), lambda o, t, s: (s[o], 0, first + t, 0)),
            whole((RW, CL)),
        ],
        [pl.BlockSpec((1, JB, TILE, NB), lambda o, t, s: (o, 0, t, 0))] * NZ,
        [pltpu.HBM((2, JB, tiles * TILE, NB), BF)] * NZ,
        (slab, k_mine),
        pick,
        flops=4 * tiles * RW * CL * NB,
    )


def gathered(slots):
    return jnp.concatenate([fold(s) for s in slots], axis=0)


def y_expand(slots, kt_mine, kt_other, pick, first, tiles):
    def body(_, *refs):
        slot_refs, (km, ko, send, kept) = refs[:NZ], refs[NZ:]
        stack = gathered([s[...] for s in slot_refs])
        send[...] = dot(ko[...], stack).reshape(LB, TILE, NB).astype(BF)
        kept[0] = dot(km[...], stack).reshape(LB, TILE, NB).astype(BF)

    return call(
        body,
        (tiles,),
        [pl.BlockSpec((JB, TILE, NB), lambda t, s: (0, t, 0))] * NZ
        + [whole((CL, RW)), whole((CL, RW))],
        [
            pl.BlockSpec((LB, TILE, NB), lambda t, s: (0, t, 0)),
            pl.BlockSpec((1, LB, TILE, NB), lambda t, s: (s[0], 0, first + t, 0)),
        ],
        [
            jax.ShapeDtypeStruct((LB, tiles * TILE, NB), BF),
            jax.ShapeDtypeStruct((2, LB, MB, NB), BF),
        ],
        (*slots, kt_mine, kt_other),
        pick,
        flops=4 * tiles * RW * CL * NB,
    )


def z_expand(slots, kt_mine, out, pick, first, tiles):
    def body(_, *refs):
        slot_refs, km, kept = refs[:NZ], refs[NZ], refs[NZ + 2]
        stack = gathered([s[0] for s in slot_refs])
        kept[0] = dot(km[...], stack).reshape(LB, TILE, NB).astype(BF)

    return call(
        body,
        (2, tiles),
        [pl.BlockSpec((1, JB, TILE, NB), lambda o, t, s: (o, 0, t, 0))] * NZ
        + [whole((CL, RW)), pl.BlockSpec(memory_space=pl.ANY)],
        pl.BlockSpec((1, LB, TILE, NB), lambda o, t, s: (s[o], 0, first + t, 0)),
        jax.ShapeDtypeStruct((2, LB, MB, NB), BF),
        (*slots, kt_mine, out),
        pick,
        {NZ + 2: 0},
        flops=4 * tiles * RW * CL * NB,
    )


def put(got, out, pick, first, tiles):
    def body(_, src, __, dst):
        dst[0] = src[...]

    return call(
        body,
        (tiles,),
        [
            pl.BlockSpec((LB, TILE, NB), lambda t, s: (0, t, 0)),
            pl.BlockSpec(memory_space=pl.ANY),
        ],
        pl.BlockSpec((1, LB, TILE, NB), lambda t, s: (s[1], 0, first + t, 0)),
        jax.ShapeDtypeStruct((2, LB, MB, NB), BF),
        (got, out),
        pick,
        {2: 0},
    )


def to_virtual(summed, v_halves):
    def body(s, v, out):
        flat = s[...].astype(F32).reshape(JB * MB, NB).astype(BF)
        out[...] = dot(flat, v[0]).reshape(JB, MB, HALF).astype(BF)

    return call(
        body,
        (2,),
        [whole((JB, MB, NB)), pl.BlockSpec((1, NB, HALF), lambda h: (h, 0, 0))],
        pl.BlockSpec((JB, MB, HALF), lambda h: (h, 0, 0)),
        jax.ShapeDtypeStruct((NROW, MB, HALF), BF),
        (summed, v_halves),
        flops=2 * JB * MB * NB * NV,
    )


def divide(second, coef, coef_t, column, row):
    def body(x, v, vt, c, r, out):
        third = dot(vt[...], x[...])
        amplitude = (third / (c[...] + r[...])).astype(BF)
        out[...] = dot(v[...], amplitude).astype(BF)

    return call(
        body,
        (1,),
        [whole((NB, HALF)), whole((NB, NV)), whole((NV, NB)), whole((NV, 1)), whole((1, HALF))],
        whole((NB, HALF)),
        jax.ShapeDtypeStruct((NB, HALF), BF),
        (second, coef, coef_t, column, row),
        flops=4 * NB * HALF * NV,
    )


def to_basis(back, vt_halves, sizes):
    def body(x, v, *outs):
        flat = [
            x[h * JB : (h + 1) * JB].astype(F32).reshape(JB * MB, HALF).astype(BF) for h in range(2)
        ]
        wide = (dot(flat[0], v[0]) + dot(flat[1], v[1])).reshape(JB, MB, NB)
        lo = 0
        for out, size in zip(outs, sizes):
            out[...] = wide[:, lo : lo + size].astype(BF)
            lo += size

    return call(
        body,
        (1,),
        [whole((NROW, MB, HALF)), whole((2, HALF, NB))],
        [whole((JB, size, NB)) for size in sizes],
        [jax.ShapeDtypeStruct((JB, size, NB), BF) for size in sizes],
        (back, vt_halves),
        flops=2 * JB * MB * NB * NV,
    )


def add(*terms):
    total = terms[0].astype(F32)
    for term in terms[1:]:
        total = total + term.astype(F32)
    return total.astype(BF)


def move(x, step):
    return lax.ppermute(x, "z", [(i, (i + step) % NZ) for i in range(NZ)])


def swap(x):
    return lax.ppermute(x, "ylo", SWAP)


def reduce_z(parts, way):
    hop = [parts[3], parts[NZ - 3]]
    far = move(parts[4], 2 * way)
    for k in (2, 1, 0):
        hop = [move(hop[0], 1), move(hop[1], -1)]
        if k:
            terms = [[hop[0], parts[k]], [hop[1], parts[NZ - k]]]
            if k == 2:
                terms[0 if way > 0 else 1].append(far)
            hop = [add(*t) for t in terms]
    return add(parts[0], *hop)


def gather_z(own, way):
    slots = [own] + [None] * (NZ - 1)
    hop = [own, own]
    for k in (1, 2, 3):
        if k == 3:
            slots[4] = move(hop[0 if way > 0 else 1], 2 * way)
        hop = [move(hop[0], 1), move(hop[1], -1)]
        slots[NZ - k], slots[k] = hop
    return slots


def run(slab, coef_virtual, coef_occupied, occ_level, virt_level, orbital_index):
    zi = lax.axis_index("z")
    yi = lax.axis_index("ylo")
    ri = lax.axis_index("row")
    slab = pltpu.with_memory_space_constraint(slab, pltpu.HBM)
    pick = jnp.stack([yi, 1 - yi]).astype(jnp.int32)
    eo = occ_level.astype(F32) / 64.0
    ev = virt_level.astype(F32) / 64.0
    occs = jnp.arange(NO, dtype=jnp.int32)
    chosen = jnp.sum(jnp.where(jnp.arange(2) == yi, orbital_index, 0))
    energy_i = jnp.sum(jnp.where(occs == chosen, eo, 0.0))
    energy_j = jnp.sum(jnp.where(occs == zi * JB + ri % JB, eo, 0.0))
    row = (jnp.where(ri // JB == 0, ev[:HALF], ev[HALF:]) - energy_i - energy_j)[None, :]
    column = ev[:, None]
    coef_t = coef_virtual.T
    v_halves = jnp.stack([coef_virtual[:, :HALF], coef_virtual[:, HALF:]])
    vt_halves = coef_t.reshape(2, HALF, NB)

    k_mine = spread(coef_occupied.T, zi * 2 * LB + yi * LB, zi)
    k_other = spread(coef_occupied.T, zi * 2 * LB + (1 - yi) * LB, zi)

    raised, held = lax.optimization_barrier((lift(slab, pick), k_mine))
    swapped = swap(raised)
    both = reduce_z(z_parts(slab, held, pick, YT, ZT), -1)
    last = add(both[0], swap(both[1]))
    lead = reduce_z(y_parts(slab, swapped, k_mine, k_other, pick, 0, YT), 1)
    summed = jnp.concatenate([lead, last], axis=1)

    first = to_virtual(summed, v_halves)
    second = lax.all_to_all(first, "row", 0, 0, tiled=True).reshape(NB, HALF)
    back_one = divide(second, coef_virtual, coef_t, column, row)
    back = lax.all_to_all(back_one.reshape(NROW, MB, HALF), "row", 0, 0, tiled=True)
    wide_y, wide_z = to_basis(back, vt_halves, (YM, ZM))

    kt_mine, kt_other = k_mine.T, k_other.T
    slots = gather_z(wide_y, 1)
    send, out = y_expand(slots, kt_mine, kt_other, pick, 0, YT)
    got = swap(send)
    both = jnp.stack([wide_z, swap(wide_z)])
    out = z_expand(gather_z(both, -1), kt_mine, out, pick, YT, ZT)
    return put(got, out, pick, 0, YT)


def solution(mesh):
    fine = Mesh(mesh.devices.reshape(NROW, NZ, 2), ("row", "z", "ylo"))
    slab = P(None, ("z", "ylo"), "row", None)
    return jax.shard_map(
        run, mesh=fine, in_specs=(slab, P(), P(), P(), P(), P()), out_specs=slab, check_vma=False
    )
```

```python
import jax
import jax.numpy as jnp
from jax import lax
from jax.experimental import pallas as pl
from jax.experimental.pallas import tpu as pltpu
from jax.sharding import Mesh, PartitionSpec as P


NB = 640
NO = 64
NV = 576
NROW = 16
NZ = 8
TILE = 8
JB = NO // NZ
LB = NB // 16
MB = NB // NROW
HALF = NV // 2
RW = NO * TILE
CL = LB * TILE
BF = jnp.bfloat16
F32 = jnp.float32
SWAP = [(0, 1), (1, 0)]
YT, ZT = 3, 2
YM, ZM = YT * TILE, ZT * TILE
LEAD = 3
FAR = NZ // 2
JH = JB // 2


def dot(a, b):
    return lax.dot_general(a, b, (((1,), (0,)), ((), ())), preferred_element_type=F32)


def call(body, grid, in_specs, out_specs, out_shape, args, scalars=None, aliases=None, flops=0):
    nbytes = sum(a.size * a.dtype.itemsize for a in args) // 2
    spec = pltpu.PrefetchScalarGridSpec(
        num_scalar_prefetch=0 if scalars is None else 1,
        grid=grid,
        in_specs=in_specs,
        out_specs=out_specs,
    )
    lead = () if scalars is None else (scalars,)
    return pl.pallas_call(
        body,
        grid_spec=spec,
        out_shape=out_shape,
        input_output_aliases=aliases or {},
        cost_estimate=pl.CostEstimate(flops=flops, bytes_accessed=nbytes, transcendentals=0),
        compiler_params=pltpu.CompilerParams(vmem_limit_bytes=24 * 1024 * 1024),
    )(*lead, *args)


def spread(coef_t, base, zi):
    lam = lax.broadcasted_iota(jnp.int32, (NB, CL), 0)
    col = lax.broadcasted_iota(jnp.int32, (NB, CL), 1)
    pick = (lam == base + col // TILE).astype(BF)
    wide = dot(coef_t, pick).astype(BF)
    row = lax.broadcasted_iota(jnp.int32, (RW, NO), 0)
    occ = lax.broadcasted_iota(jnp.int32, (RW, NO), 1)
    block = row // TILE
    want = ((zi + block // JB + LEAD) % NZ) * JB + block % JB
    tall = dot((occ == want).astype(BF), wide)
    row = lax.broadcasted_iota(jnp.int32, (RW, CL), 0)
    col = lax.broadcasted_iota(jnp.int32, (RW, CL), 1)
    return jnp.where(row % TILE == col % TILE, tall, 0.0).astype(BF)


def fold(x):
    return x.astype(F32).reshape(x.shape[0] * x.shape[1], x.shape[2]).astype(BF)


def whole(shape):
    return pl.BlockSpec(shape, lambda *_: (0,) * len(shape))


def lift(slab, pick):
    step = 20

    def body(_, src, dst):
        dst[...] = src[0]

    return call(
        body,
        (LB // step,),
        [pl.BlockSpec((1, step, YM, NB), lambda i, s: (s[1], i, 0, 0))],
        pl.BlockSpec((step, YM, NB), lambda i, s: (i, 0, 0)),
        jax.ShapeDtypeStruct((LB, YM, NB), BF),
        (slab,),
        pick,
    )


def y_parts(slab, swapped, k_mine, k_other, pick, first, tiles, lo, hi):
    rows = slice(lo * JB * TILE, hi * JB * TILE)

    def body(_, here, came, km, ko, *outs):
        part = dot(km[rows], fold(here[0])) + dot(ko[rows], fold(came[...]))
        part = part.reshape(hi - lo, JB, TILE, NB)
        for k, out in enumerate(outs):
            out[...] = part[k].astype(BF)

    return call(
        body,
        (tiles,),
        [
            pl.BlockSpec((1, LB, TILE, NB), lambda t, s: (s[0], 0, first + t, 0)),
            pl.BlockSpec((LB, TILE, NB), lambda t, s: (0, t, 0)),
            whole((RW, CL)),
            whole((RW, CL)),
        ],
        [pl.BlockSpec((JB, TILE, NB), lambda t, s: (0, t, 0))] * (hi - lo),
        [jax.ShapeDtypeStruct((JB, tiles * TILE, NB), BF)] * (hi - lo),
        (slab, swapped, k_mine, k_other),
        pick,
        flops=4 * tiles * (hi - lo) * JB * TILE * CL * NB,
    )


def z_parts(slab, k_mine, pick, first, tiles, lo, hi):
    rows = slice(lo * JB * TILE, hi * JB * TILE)

    def body(_, here, km, *outs):
        part = dot(km[rows], fold(here[0])).reshape(hi - lo, JB, TILE, NB)
        for k, out in enumerate(outs):
            out[0] = part[k].astype(BF)

    return call(
        body,
        (2, tiles),
        [
            pl.BlockSpec((1, LB, TILE, NB), lambda o, t, s: (s[o], 0, first + t, 0)),
            whole((RW, CL)),
        ],
        [pl.BlockSpec((1, JB, TILE, NB), lambda o, t, s: (o, 0, t, 0))] * (hi - lo),
        [pltpu.HBM((2, JB, tiles * TILE, NB), BF)] * (hi - lo),
        (slab, k_mine),
        pick,
        flops=4 * tiles * (hi - lo) * JB * TILE * CL * NB,
    )


def gathered(slots):
    return jnp.concatenate([fold(s) for s in slots], axis=0)


def rolled(slots):
    return [*slots[LEAD:], *slots[:LEAD]]


def y_expand(slots, kt_mine, kt_other, pick, first, tiles):
    def body(_, *refs):
        slot_refs, (km, ko, send, kept) = refs[: len(slots)], refs[len(slots) :]
        stack = gathered([s[...] for s in slot_refs])
        send[...] = dot(ko[...], stack).reshape(LB, TILE, NB).astype(BF)
        kept[0] = dot(km[...], stack).reshape(LB, TILE, NB).astype(BF)

    return call(
        body,
        (tiles,),
        [pl.BlockSpec((s.shape[0], TILE, NB), lambda t, s: (0, t, 0)) for s in slots]
        + [whole((CL, RW)), whole((CL, RW))],
        [
            pl.BlockSpec((LB, TILE, NB), lambda t, s: (0, t, 0)),
            pl.BlockSpec((1, LB, TILE, NB), lambda t, s: (s[0], 0, first + t, 0)),
        ],
        [
            jax.ShapeDtypeStruct((LB, tiles * TILE, NB), BF),
            jax.ShapeDtypeStruct((2, LB, MB, NB), BF),
        ],
        (*slots, kt_mine, kt_other),
        pick,
        flops=4 * tiles * RW * CL * NB,
    )


def z_expand(slots, kt_mine, out, pick, first, tiles):
    def body(_, *refs):
        slot_refs, km, kept = refs[:NZ], refs[NZ], refs[NZ + 2]
        stack = gathered([s[0] for s in slot_refs])
        kept[0] = dot(km[...], stack).reshape(LB, TILE, NB).astype(BF)

    return call(
        body,
        (2, tiles),
        [pl.BlockSpec((1, JB, TILE, NB), lambda o, t, s: (o, 0, t, 0))] * NZ
        + [whole((CL, RW)), pl.BlockSpec(memory_space=pl.ANY)],
        pl.BlockSpec((1, LB, TILE, NB), lambda o, t, s: (s[o], 0, first + t, 0)),
        jax.ShapeDtypeStruct((2, LB, MB, NB), BF),
        (*slots, kt_mine, out),
        pick,
        {NZ + 2: 0},
        flops=4 * tiles * RW * CL * NB,
    )


def put(got, out, pick, first, tiles):
    def body(_, src, __, dst):
        dst[0] = src[...]

    return call(
        body,
        (tiles,),
        [
            pl.BlockSpec((LB, TILE, NB), lambda t, s: (0, t, 0)),
            pl.BlockSpec(memory_space=pl.ANY),
        ],
        pl.BlockSpec((1, LB, TILE, NB), lambda t, s: (s[1], 0, first + t, 0)),
        jax.ShapeDtypeStruct((2, LB, MB, NB), BF),
        (got, out),
        pick,
        {2: 0},
    )


def to_virtual(summed, v_halves):
    def body(s, v, out):
        flat = s[...].astype(F32).reshape(JB * MB, NB).astype(BF)
        out[...] = dot(flat, v[0]).reshape(JB, MB, HALF).astype(BF)

    return call(
        body,
        (2,),
        [whole((JB, MB, NB)), pl.BlockSpec((1, NB, HALF), lambda h: (h, 0, 0))],
        pl.BlockSpec((JB, MB, HALF), lambda h: (h, 0, 0)),
        jax.ShapeDtypeStruct((NROW, MB, HALF), BF),
        (summed, v_halves),
        flops=2 * JB * MB * NB * NV,
    )


def divide(second, coef, coef_t, column, row):
    def body(x, v, vt, c, r, out):
        third = dot(vt[...], x[...])
        amplitude = (third / (c[...] + r[...])).astype(BF)
        out[...] = dot(v[...], amplitude).astype(BF)

    return call(
        body,
        (1,),
        [whole((NB, HALF)), whole((NB, NV)), whole((NV, NB)), whole((NV, 1)), whole((1, HALF))],
        whole((NB, HALF)),
        jax.ShapeDtypeStruct((NB, HALF), BF),
        (second, coef, coef_t, column, row),
        flops=4 * NB * HALF * NV,
    )


def to_basis(back, vt_halves, sizes):
    def body(x, v, *outs):
        flat = [
            x[h * JB : (h + 1) * JB].astype(F32).reshape(JB * MB, HALF).astype(BF) for h in range(2)
        ]
        wide = (dot(flat[0], v[0]) + dot(flat[1], v[1])).reshape(JB, MB, NB)
        lo = 0
        for out, size in zip(outs, sizes):
            out[...] = wide[:, lo : lo + size].astype(BF)
            lo += size

    return call(
        body,
        (1,),
        [whole((NROW, MB, HALF)), whole((2, HALF, NB))],
        [whole((JB, size, NB)) for size in sizes],
        [jax.ShapeDtypeStruct((JB, size, NB), BF) for size in sizes],
        (back, vt_halves),
        flops=2 * JB * MB * NB * NV,
    )


def add(*terms):
    total = terms[0].astype(F32)
    for term in terms[1:]:
        total = total + term.astype(F32)
    return total.astype(BF)


def move(x, step):
    return lax.ppermute(x, "z", [(i, (i + step) % NZ) for i in range(NZ)])


def swap(x):
    return lax.ppermute(x, "ylo", SWAP)


def unrolled(parts):
    return [*parts[NZ - LEAD :], *parts[: NZ - LEAD]]


def chain_sum(parts):
    up, down = parts[3], parts[FAR]
    for n in range(1, FAR + 1):
        if n < FAR:
            up = move(up, 1)
            up = add(up, parts[3 - n]) if n < 3 else up
        down = move(down, -1)
        down = add(down, parts[FAR + n]) if n < FAR else down
    return add(parts[0], up, down)


def tree_sum(parts):
    up = move(parts[3], 1)
    down = move(parts[5], -1)
    high = move(parts[FAR][:JH], 2)
    low = move(parts[FAR][JH:], -2)
    none = jnp.zeros_like(high)
    up = add(up, parts[2], jnp.concatenate([high, none], axis=0))
    down = add(down, parts[6], jnp.concatenate([none, low], axis=0))
    up = add(move(up, 1), parts[1])
    down = add(move(down, -1), parts[7])
    return add(parts[0], move(up, 1), move(down, -1))


def chain_gather(own):
    slots = [own] + [None] * (NZ - 1)
    up = down = own
    for n in range(1, FAR + 1):
        if n < FAR:
            up = slots[NZ - n] = move(up, 1)
        down = slots[n] = move(down, -1)
    return rolled(slots)


def tree_gather(own):
    up1 = move(own, 1)
    down1 = move(own, -1)
    up2 = move(up1, 1)
    down2 = move(down1, -1)
    up3 = move(up2, 1)
    down3 = move(down2, -1)
    high = move(up2[:JH], 2)
    low = move(down2[JH:], -2)
    return [down3, high, low, up3, up2, up1, own, down1, down2]


def run(slab, coef_virtual, coef_occupied, occ_level, virt_level, orbital_index):
    zi = lax.axis_index("z")
    yi = lax.axis_index("ylo")
    ri = lax.axis_index("row")
    slab = pltpu.with_memory_space_constraint(slab, pltpu.HBM)
    pick = jnp.stack([yi, 1 - yi]).astype(jnp.int32)
    eo = occ_level.astype(F32) / 64.0
    ev = virt_level.astype(F32) / 64.0
    occs = jnp.arange(NO, dtype=jnp.int32)
    chosen = jnp.sum(jnp.where(jnp.arange(2) == yi, orbital_index, 0))
    energy_i = jnp.sum(jnp.where(occs == chosen, eo, 0.0))
    energy_j = jnp.sum(jnp.where(occs == zi * JB + ri % JB, eo, 0.0))
    row = (jnp.where(ri // JB == 0, ev[:HALF], ev[HALF:]) - energy_i - energy_j)[None, :]
    column = ev[:, None]
    coef_t = coef_virtual.T
    v_halves = jnp.stack([coef_virtual[:, :HALF], coef_virtual[:, HALF:]])
    vt_halves = coef_t.reshape(2, HALF, NB)

    k_mine = spread(coef_occupied.T, zi * 2 * LB + yi * LB, zi)
    k_other = spread(coef_occupied.T, zi * 2 * LB + (1 - yi) * LB, zi)

    raised, held = lax.optimization_barrier((lift(slab, pick), k_mine))
    swapped = swap(raised)
    head = z_parts(slab, held, pick, YT, ZT, 0, 2)
    tail = z_parts(slab, held, pick, YT, ZT, 2, NZ)
    both = chain_sum(unrolled([*head, *tail]))
    last = add(both[0], swap(both[1]))
    head = y_parts(slab, swapped, k_mine, k_other, pick, 0, YT, 0, 3)
    tail = y_parts(slab, swapped, k_mine, k_other, pick, 0, YT, 3, NZ)
    lead = tree_sum(unrolled([*head, *tail]))
    summed = jnp.concatenate([lead, last], axis=1)

    first = to_virtual(summed, v_halves)
    second = lax.all_to_all(first, "row", 0, 0, tiled=True).reshape(NB, HALF)
    back_one = divide(second, coef_virtual, coef_t, column, row)
    back = lax.all_to_all(back_one.reshape(NROW, MB, HALF), "row", 0, 0, tiled=True)
    wide_y, wide_z = to_basis(back, vt_halves, (YM, ZM))

    kt_mine, kt_other = k_mine.T, k_other.T
    slots = tree_gather(wide_y)
    send, out = y_expand(slots, kt_mine, kt_other, pick, 0, YT)
    got = swap(send)
    both = jnp.stack([wide_z, swap(wide_z)])
    out = z_expand(chain_gather(both), kt_mine, out, pick, YT, ZT)
    return put(got, out, pick, 0, YT)


def solution(mesh):
    fine = Mesh(mesh.devices.reshape(NROW, NZ, 2), ("row", "z", "ylo"))
    slab = P(None, ("z", "ylo"), "row", None)
    return jax.shard_map(
        run, mesh=fine, in_specs=(slab, P(), P(), P(), P(), P()), out_specs=slab, check_vma=False
    )
```

```python
import jax
import jax.numpy as jnp
from jax import lax
from jax.experimental import pallas as pl
from jax.experimental.pallas import tpu as pltpu
from jax.sharding import Mesh, PartitionSpec as P


NB = 640
NO = 64
NV = 576
NROW = 16
NZ = 8
TILE = 8
JB = NO // NZ
LB = NB // 16
MB = NB // NROW
HALF = NV // 2
RW = NO * TILE
CL = LB * TILE
BF = jnp.bfloat16
F32 = jnp.float32
SWAP = [(0, 1), (1, 0)]
YT, ZT = 3, 2
YM, ZM = YT * TILE, ZT * TILE
LEAD = 3
FAR = NZ // 2
JH = JB // 2


def dot(a, b):
    return lax.dot_general(a, b, (((1,), (0,)), ((), ())), preferred_element_type=F32)


def call(body, grid, in_specs, out_specs, out_shape, args, scalars=None, aliases=None, flops=0):
    nbytes = sum(a.size * a.dtype.itemsize for a in args) // 2
    spec = pltpu.PrefetchScalarGridSpec(
        num_scalar_prefetch=0 if scalars is None else 1,
        grid=grid,
        in_specs=in_specs,
        out_specs=out_specs,
    )
    lead = () if scalars is None else (scalars,)
    return pl.pallas_call(
        body,
        grid_spec=spec,
        out_shape=out_shape,
        input_output_aliases=aliases or {},
        cost_estimate=pl.CostEstimate(flops=flops, bytes_accessed=nbytes, transcendentals=0),
        compiler_params=pltpu.CompilerParams(vmem_limit_bytes=24 * 1024 * 1024),
    )(*lead, *args)


def spread(coef_t, base, zi):
    lam = lax.broadcasted_iota(jnp.int32, (NB, CL), 0)
    col = lax.broadcasted_iota(jnp.int32, (NB, CL), 1)
    pick = (lam == base + col // TILE).astype(BF)
    wide = dot(coef_t, pick).astype(BF)
    row = lax.broadcasted_iota(jnp.int32, (RW, NO), 0)
    occ = lax.broadcasted_iota(jnp.int32, (RW, NO), 1)
    block = row // TILE
    want = ((zi + block // JB + LEAD) % NZ) * JB + block % JB
    tall = dot((occ == want).astype(BF), wide)
    row = lax.broadcasted_iota(jnp.int32, (RW, CL), 0)
    col = lax.broadcasted_iota(jnp.int32, (RW, CL), 1)
    return jnp.where(row % TILE == col % TILE, tall, 0.0).astype(BF)


def fold(x):
    return x.astype(F32).reshape(x.shape[0] * x.shape[1], x.shape[2]).astype(BF)


def whole(shape):
    return pl.BlockSpec(shape, lambda *_: (0,) * len(shape))


def lift(slab, pick):
    def body(which, src, dst, sem):
        copy = pltpu.make_async_copy(src.at[which[1], :, pl.ds(0, YM), :], dst, sem)
        copy.start()
        copy.wait()

    return pl.pallas_call(
        body,
        in_specs=[pl.BlockSpec(memory_space=pltpu.SMEM), pl.BlockSpec(memory_space=pltpu.HBM)],
        out_specs=pl.BlockSpec(memory_space=pltpu.VMEM),
        out_shape=pltpu.VMEM((LB, YM, NB), BF),
        scratch_shapes=[pltpu.SemaphoreType.DMA],
        name="lift",
        cost_estimate=pl.CostEstimate(flops=0, bytes_accessed=4 * LB * YM * NB, transcendentals=0),
        compiler_params=pltpu.CompilerParams(vmem_limit_bytes=24 * 1024 * 1024),
    )(pick, slab)


def y_parts(slab, swapped, k_mine, k_other, pick, first, tiles, lo, hi):
    rows = slice(lo * JB * TILE, hi * JB * TILE)

    def body(_, here, came, km, ko, *outs):
        part = dot(km[rows], fold(here[0])) + dot(ko[rows], fold(came[...]))
        part = part.reshape(hi - lo, JB, TILE, NB)
        for k, out in enumerate(outs):
            out[...] = part[k].astype(BF)

    return call(
        body,
        (tiles,),
        [
            pl.BlockSpec((1, LB, TILE, NB), lambda t, s: (s[0], 0, first + t, 0)),
            pl.BlockSpec((LB, TILE, NB), lambda t, s: (0, t, 0)),
            whole((RW, CL)),
            whole((RW, CL)),
        ],
        [pl.BlockSpec((JB, TILE, NB), lambda t, s: (0, t, 0))] * (hi - lo),
        [jax.ShapeDtypeStruct((JB, tiles * TILE, NB), BF)] * (hi - lo),
        (slab, swapped, k_mine, k_other),
        pick,
        flops=4 * tiles * (hi - lo) * JB * TILE * CL * NB,
    )


def z_parts(slab, k_mine, pick, first, tiles, lo, hi):
    rows = slice(lo * JB * TILE, hi * JB * TILE)

    def body(_, here, km, *outs):
        part = dot(km[rows], fold(here[0])).reshape(hi - lo, JB, TILE, NB)
        for k, out in enumerate(outs):
            out[0] = part[k].astype(BF)

    return call(
        body,
        (2, tiles),
        [
            pl.BlockSpec((1, LB, TILE, NB), lambda o, t, s: (s[o], 0, first + t, 0)),
            whole((RW, CL)),
        ],
        [pl.BlockSpec((1, JB, TILE, NB), lambda o, t, s: (o, 0, t, 0))] * (hi - lo),
        [jax.ShapeDtypeStruct((2, JB, tiles * TILE, NB), BF)] * (hi - lo),
        (slab, k_mine),
        pick,
        flops=4 * tiles * (hi - lo) * JB * TILE * CL * NB,
    )


def gathered(slots):
    return jnp.concatenate([fold(s) for s in slots], axis=0)


def rolled(slots):
    return [*slots[LEAD:], *slots[:LEAD]]


def y_expand(slots, kt_mine, kt_other, pick, first, tiles):
    def body(_, *refs):
        slot_refs, (km, ko, send, kept) = refs[: len(slots)], refs[len(slots) :]
        stack = gathered([s[...] for s in slot_refs])
        send[...] = dot(ko[...], stack).reshape(LB, TILE, NB).astype(BF)
        kept[0] = dot(km[...], stack).reshape(LB, TILE, NB).astype(BF)

    return call(
        body,
        (tiles,),
        [pl.BlockSpec((s.shape[0], TILE, NB), lambda t, s: (0, t, 0)) for s in slots]
        + [whole((CL, RW)), whole((CL, RW))],
        [
            pl.BlockSpec((LB, TILE, NB), lambda t, s: (0, t, 0)),
            pl.BlockSpec((1, LB, TILE, NB), lambda t, s: (s[0], 0, first + t, 0)),
        ],
        [
            jax.ShapeDtypeStruct((LB, tiles * TILE, NB), BF),
            jax.ShapeDtypeStruct((2, LB, MB, NB), BF),
        ],
        (*slots, kt_mine, kt_other),
        pick,
        flops=4 * tiles * RW * CL * NB,
    )


def z_expand(slots, kt_mine, out, pick, first, tiles):
    def body(_, *refs):
        slot_refs, km, kept = refs[:NZ], refs[NZ], refs[NZ + 2]
        stack = gathered([s[0] for s in slot_refs])
        kept[0] = dot(km[...], stack).reshape(LB, TILE, NB).astype(BF)

    return call(
        body,
        (2, tiles),
        [pl.BlockSpec((1, JB, TILE, NB), lambda o, t, s: (o, 0, t, 0))] * NZ
        + [whole((CL, RW)), pl.BlockSpec(memory_space=pl.ANY)],
        pl.BlockSpec((1, LB, TILE, NB), lambda o, t, s: (s[o], 0, first + t, 0)),
        jax.ShapeDtypeStruct((2, LB, MB, NB), BF),
        (*slots, kt_mine, out),
        pick,
        {NZ + 2: 0},
        flops=4 * tiles * RW * CL * NB,
    )


def put(got, out, pick):
    def body(which, src, _, dst, sem):
        copy = pltpu.make_async_copy(src, dst.at[which[1], :, pl.ds(0, YM), :], sem)
        copy.start()
        copy.wait()

    return pl.pallas_call(
        body,
        in_specs=[
            pl.BlockSpec(memory_space=pltpu.SMEM),
            pl.BlockSpec(memory_space=pltpu.VMEM),
            pl.BlockSpec(memory_space=pltpu.HBM),
        ],
        out_specs=pl.BlockSpec(memory_space=pltpu.HBM),
        out_shape=jax.ShapeDtypeStruct((2, LB, MB, NB), BF),
        scratch_shapes=[pltpu.SemaphoreType.DMA],
        input_output_aliases={2: 0},
        name="put",
        cost_estimate=pl.CostEstimate(flops=0, bytes_accessed=4 * LB * YM * NB, transcendentals=0),
        compiler_params=pltpu.CompilerParams(vmem_limit_bytes=24 * 1024 * 1024),
    )(pick, got, out)


def to_virtual(summed, v_halves):
    def body(s, v, out):
        flat = s[...].astype(F32).reshape(JB * MB, NB).astype(BF)
        out[...] = dot(flat, v[0]).reshape(JB, MB, HALF).astype(BF)

    return call(
        body,
        (2,),
        [whole((JB, MB, NB)), pl.BlockSpec((1, NB, HALF), lambda h: (h, 0, 0))],
        pl.BlockSpec((JB, MB, HALF), lambda h: (h, 0, 0)),
        jax.ShapeDtypeStruct((NROW, MB, HALF), BF),
        (summed, v_halves),
        flops=2 * JB * MB * NB * NV,
    )


def divide(second, coef, coef_t, column, row):
    def body(x, v, vt, c, r, out):
        third = dot(vt[...], x[...])
        amplitude = (third / (c[...] + r[...])).astype(BF)
        out[...] = dot(v[...], amplitude).astype(BF)

    return call(
        body,
        (1,),
        [whole((NB, HALF)), whole((NB, NV)), whole((NV, NB)), whole((NV, 1)), whole((1, HALF))],
        whole((NB, HALF)),
        jax.ShapeDtypeStruct((NB, HALF), BF),
        (second, coef, coef_t, column, row),
        flops=4 * NB * HALF * NV,
    )


def to_basis(back, vt_halves, sizes):
    def body(x, v, *outs):
        flat = [
            x[h * JB : (h + 1) * JB].astype(F32).reshape(JB * MB, HALF).astype(BF) for h in range(2)
        ]
        wide = (dot(flat[0], v[0]) + dot(flat[1], v[1])).reshape(JB, MB, NB)
        lo = 0
        for out, size in zip(outs, sizes):
            out[...] = wide[:, lo : lo + size].astype(BF)
            lo += size

    return call(
        body,
        (1,),
        [whole((NROW, MB, HALF)), whole((2, HALF, NB))],
        [whole((JB, size, NB)) for size in sizes],
        [jax.ShapeDtypeStruct((JB, size, NB), BF) for size in sizes],
        (back, vt_halves),
        flops=2 * JB * MB * NB * NV,
    )


def add(*terms):
    total = terms[0].astype(F32)
    for term in terms[1:]:
        total = total + term.astype(F32)
    return total.astype(BF)


def move(x, step):
    return lax.ppermute(x, "z", [(i, (i + step) % NZ) for i in range(NZ)])


def swap(x):
    return lax.ppermute(x, "ylo", SWAP)


def unrolled(parts):
    return [*parts[NZ - LEAD :], *parts[: NZ - LEAD]]


def chain_sum(parts):
    up, down = parts[3], parts[FAR]
    for n in range(1, FAR + 1):
        if n < FAR:
            up = move(up, 1)
            up = add(up, parts[3 - n]) if n < 3 else up
        down = move(down, -1)
        down = add(down, parts[FAR + n]) if n < FAR else down
    return add(parts[0], up, down)


def tree_sum(parts):
    up = move(parts[3], 1)
    down = move(parts[5], -1)
    high = move(parts[FAR][:JH], 2)
    low = move(parts[FAR][JH:], -2)
    none = jnp.zeros_like(high)
    up = add(up, parts[2], jnp.concatenate([high, none], axis=0))
    down = add(down, parts[6], jnp.concatenate([none, low], axis=0))
    up = add(move(up, 1), parts[1])
    down = add(move(down, -1), parts[7])
    return add(parts[0], move(up, 1), move(down, -1))


def chain_gather(own):
    slots = [own] + [None] * (NZ - 1)
    up = down = own
    for n in range(1, FAR + 1):
        if n < FAR:
            up = slots[NZ - n] = move(up, 1)
        down = slots[n] = move(down, -1)
    return rolled(slots)


def tree_gather(own):
    up1 = move(own, 1)
    down1 = move(own, -1)
    up2 = move(up1, 1)
    down2 = move(down1, -1)
    up3 = move(up2, 1)
    down3 = move(down2, -1)
    high = move(up2[:JH], 2)
    low = move(down2[JH:], -2)
    return [down3, high, low, up3, up2, up1, own, down1, down2]


def run(slab, coef_virtual, coef_occupied, occ_level, virt_level, orbital_index):
    zi = lax.axis_index("z")
    yi = lax.axis_index("ylo")
    ri = lax.axis_index("row")
    slab = pltpu.with_memory_space_constraint(slab, pltpu.HBM)
    pick = jnp.stack([yi, 1 - yi]).astype(jnp.int32)
    eo = occ_level.astype(F32) / 64.0
    ev = virt_level.astype(F32) / 64.0
    occs = jnp.arange(NO, dtype=jnp.int32)
    chosen = jnp.sum(jnp.where(jnp.arange(2) == yi, orbital_index, 0))
    energy_i = jnp.sum(jnp.where(occs == chosen, eo, 0.0))
    energy_j = jnp.sum(jnp.where(occs == zi * JB + ri % JB, eo, 0.0))
    row = (jnp.where(ri // JB == 0, ev[:HALF], ev[HALF:]) - energy_i - energy_j)[None, :]
    column = ev[:, None]
    coef_t = coef_virtual.T
    v_halves = jnp.stack([coef_virtual[:, :HALF], coef_virtual[:, HALF:]])
    vt_halves = coef_t.reshape(2, HALF, NB)

    raised, coef_o = lax.optimization_barrier((lift(slab, pick), coef_occupied.T))
    swapped = swap(raised)
    k_mine = spread(coef_o, zi * 2 * LB + yi * LB, zi)
    k_other = spread(coef_o, zi * 2 * LB + (1 - yi) * LB, zi)
    head = z_parts(slab, k_mine, pick, YT, ZT, 0, 2)
    tail = z_parts(slab, k_mine, pick, YT, ZT, 2, NZ)
    both = chain_sum(unrolled([*head, *tail]))
    last = add(both[0], swap(both[1]))
    head = y_parts(slab, swapped, k_mine, k_other, pick, 0, YT, 0, 3)
    tail = y_parts(slab, swapped, k_mine, k_other, pick, 0, YT, 3, NZ)
    lead = tree_sum(unrolled([*head, *tail]))
    summed = jnp.concatenate([lead, last], axis=1)

    first = to_virtual(summed, v_halves)
    second = lax.all_to_all(first, "row", 0, 0, tiled=True).reshape(NB, HALF)
    back_one = divide(second, coef_virtual, coef_t, column, row)
    back = lax.all_to_all(back_one.reshape(NROW, MB, HALF), "row", 0, 0, tiled=True)
    wide_y, wide_z = to_basis(back, vt_halves, (YM, ZM))

    kt_mine, kt_other = k_mine.T, k_other.T
    slots = tree_gather(wide_y)
    send, out = y_expand(slots, kt_mine, kt_other, pick, 0, YT)
    got = swap(send)
    both = jnp.stack([wide_z, swap(wide_z)])
    out = z_expand(chain_gather(both), kt_mine, out, pick, YT, ZT)
    return put(got, out, pick)


def solution(mesh):
    fine = Mesh(mesh.devices.reshape(NROW, NZ, 2), ("row", "z", "ylo"))
    slab = P(None, ("z", "ylo"), "row", None)
    return jax.shard_map(
        run, mesh=fine, in_specs=(slab, P(), P(), P(), P(), P()), out_specs=slab, check_vma=False
    )
```

```python
import jax
import jax.numpy as jnp
from jax import lax
from jax.experimental import pallas as pl
from jax.experimental.pallas import tpu as pltpu
from jax.sharding import Mesh, PartitionSpec as P


NB = 640
NO = 64
NV = 576
NROW = 16
NZ = 8
TILE = 8
JB = NO // NZ
LB = NB // 16
MB = NB // NROW
HALF = NV // 2
RW = NO * TILE
CL = LB * TILE
BF = jnp.bfloat16
F32 = jnp.float32
SWAP = [(0, 1), (1, 0)]
YT, ZT = 3, 2
YM, ZM = YT * TILE, ZT * TILE
LEAD = 3
FAR = NZ // 2
JH = JB // 2


def dot(a, b):
    return lax.dot_general(a, b, (((1,), (0,)), ((), ())), preferred_element_type=F32)


def call(body, grid, in_specs, out_specs, out_shape, args, scalars=None, aliases=None, flops=0):
    nbytes = sum(a.size * a.dtype.itemsize for a in args) // 2
    spec = pltpu.PrefetchScalarGridSpec(
        num_scalar_prefetch=0 if scalars is None else 1,
        grid=grid,
        in_specs=in_specs,
        out_specs=out_specs,
    )
    lead = () if scalars is None else (scalars,)
    return pl.pallas_call(
        body,
        grid_spec=spec,
        out_shape=out_shape,
        input_output_aliases=aliases or {},
        cost_estimate=pl.CostEstimate(flops=flops, bytes_accessed=nbytes, transcendentals=0),
        compiler_params=pltpu.CompilerParams(vmem_limit_bytes=24 * 1024 * 1024),
    )(*lead, *args)


def spread(coef_t, base, zi):
    lam = lax.broadcasted_iota(jnp.int32, (NB, CL), 0)
    col = lax.broadcasted_iota(jnp.int32, (NB, CL), 1)
    pick = (lam == base + col // TILE).astype(BF)
    wide = dot(coef_t, pick).astype(BF)
    row = lax.broadcasted_iota(jnp.int32, (RW, NO), 0)
    occ = lax.broadcasted_iota(jnp.int32, (RW, NO), 1)
    block = row // TILE
    want = ((zi + block // JB + LEAD) % NZ) * JB + block % JB
    tall = dot((occ == want).astype(BF), wide)
    row = lax.broadcasted_iota(jnp.int32, (RW, CL), 0)
    col = lax.broadcasted_iota(jnp.int32, (RW, CL), 1)
    return jnp.where(row % TILE == col % TILE, tall, 0.0).astype(BF)


def fold(x):
    return x.astype(F32).reshape(x.shape[0] * x.shape[1], x.shape[2]).astype(BF)


def whole(shape):
    return pl.BlockSpec(shape, lambda *_: (0,) * len(shape))


CUTS = 5
CUT = LB // CUTS


def lift(slab, pick):
    def body(which, src, dst, hold, came, went):
        def spot(i):
            return pl.ds(i * CUT, CUT)

        takes = [
            pltpu.make_async_copy(
                src.at[which[1], spot(i), pl.ds(0, YM), :], hold.at[spot(i)], came.at[i]
            )
            for i in range(CUTS)
        ]
        gives = [
            pltpu.make_async_copy(hold.at[spot(i)], dst.at[spot(i)], went.at[i])
            for i in range(CUTS)
        ]
        for take in takes:
            take.start()
        for take, give in zip(takes, gives):
            take.wait()
            give.start()
        for give in gives:
            give.wait()

    return pl.pallas_call(
        body,
        in_specs=[pl.BlockSpec(memory_space=pltpu.SMEM), pl.BlockSpec(memory_space=pltpu.HBM)],
        out_specs=pl.BlockSpec(memory_space=pltpu.HBM),
        out_shape=jax.ShapeDtypeStruct((LB, YM, NB), BF),
        scratch_shapes=[
            pltpu.VMEM((LB, YM, NB), BF),
            pltpu.SemaphoreType.DMA((CUTS,)),
            pltpu.SemaphoreType.DMA((CUTS,)),
        ],
        name="lift",
        cost_estimate=pl.CostEstimate(flops=0, bytes_accessed=4 * LB * YM * NB, transcendentals=0),
        compiler_params=pltpu.CompilerParams(vmem_limit_bytes=24 * 1024 * 1024),
    )(pick, slab)


def y_parts(slab, swapped, k_mine, k_other, pick, first, tiles, lo, hi):
    rows = slice(lo * JB * TILE, hi * JB * TILE)

    def body(_, here, came, km, ko, *outs):
        part = dot(km[rows], fold(here[0])) + dot(ko[rows], fold(came[...]))
        part = part.reshape(hi - lo, JB, TILE, NB)
        for k, out in enumerate(outs):
            out[...] = part[k].astype(BF)

    return call(
        body,
        (tiles,),
        [
            pl.BlockSpec((1, LB, TILE, NB), lambda t, s: (s[0], 0, first + t, 0)),
            pl.BlockSpec((LB, TILE, NB), lambda t, s: (0, t, 0)),
            whole((RW, CL)),
            whole((RW, CL)),
        ],
        [pl.BlockSpec((JB, TILE, NB), lambda t, s: (0, t, 0))] * (hi - lo),
        [jax.ShapeDtypeStruct((JB, tiles * TILE, NB), BF)] * (hi - lo),
        (slab, swapped, k_mine, k_other),
        pick,
        flops=4 * tiles * (hi - lo) * JB * TILE * CL * NB,
    )


def z_parts(slab, k_mine, pick, first, tiles, lo, hi):
    rows = slice(lo * JB * TILE, hi * JB * TILE)

    def body(_, here, km, *outs):
        part = dot(km[rows], fold(here[0])).reshape(hi - lo, JB, TILE, NB)
        for k, out in enumerate(outs):
            out[0] = part[k].astype(BF)

    return call(
        body,
        (2, tiles),
        [
            pl.BlockSpec((1, LB, TILE, NB), lambda o, t, s: (s[o], 0, first + t, 0)),
            whole((RW, CL)),
        ],
        [pl.BlockSpec((1, JB, TILE, NB), lambda o, t, s: (o, 0, t, 0))] * (hi - lo),
        [jax.ShapeDtypeStruct((2, JB, tiles * TILE, NB), BF)] * (hi - lo),
        (slab, k_mine),
        pick,
        flops=4 * tiles * (hi - lo) * JB * TILE * CL * NB,
    )


def gathered(slots):
    return jnp.concatenate([fold(s) for s in slots], axis=0)


def rolled(slots):
    return [*slots[LEAD:], *slots[:LEAD]]


def y_send(slots, kt_other, tiles):
    def body(*refs):
        slot_refs, (ko, send) = refs[: len(slots)], refs[len(slots) :]
        stack = gathered([s[...] for s in slot_refs])
        send[...] = dot(ko[...], stack).reshape(LB, TILE, NB).astype(BF)

    return call(
        body,
        (tiles,),
        [pl.BlockSpec((s.shape[0], TILE, NB), lambda t: (0, t, 0)) for s in slots]
        + [whole((CL, RW))],
        pl.BlockSpec((LB, TILE, NB), lambda t: (0, t, 0)),
        jax.ShapeDtypeStruct((LB, tiles * TILE, NB), BF),
        (*slots, kt_other),
        flops=2 * tiles * RW * CL * NB,
    )


def y_keep(slots, kt_mine, pick, first, tiles):
    def body(_, *refs):
        slot_refs, (km, kept) = refs[: len(slots)], refs[len(slots) :]
        stack = gathered([s[...] for s in slot_refs])
        kept[0] = dot(km[...], stack).reshape(LB, TILE, NB).astype(BF)

    return call(
        body,
        (tiles,),
        [pl.BlockSpec((s.shape[0], TILE, NB), lambda t, s: (0, t, 0)) for s in slots]
        + [whole((CL, RW))],
        pl.BlockSpec((1, LB, TILE, NB), lambda t, s: (s[0], 0, first + t, 0)),
        jax.ShapeDtypeStruct((2, LB, MB, NB), BF),
        (*slots, kt_mine),
        pick,
        flops=2 * tiles * RW * CL * NB,
    )


def z_expand(slots, kt_mine, out, pick, first, tiles):
    def body(_, *refs):
        slot_refs, km, kept = refs[:NZ], refs[NZ], refs[NZ + 2]
        stack = gathered([s[0] for s in slot_refs])
        kept[0] = dot(km[...], stack).reshape(LB, TILE, NB).astype(BF)

    return call(
        body,
        (2, tiles),
        [pl.BlockSpec((1, JB, TILE, NB), lambda o, t, s: (o, 0, t, 0))] * NZ
        + [whole((CL, RW)), pl.BlockSpec(memory_space=pl.ANY)],
        pl.BlockSpec((1, LB, TILE, NB), lambda o, t, s: (s[o], 0, first + t, 0)),
        jax.ShapeDtypeStruct((2, LB, MB, NB), BF),
        (*slots, kt_mine, out),
        pick,
        {NZ + 2: 0},
        flops=4 * tiles * RW * CL * NB,
    )


def put(got, out, pick):
    def body(which, src, _, dst, sem):
        copies = [
            pltpu.make_async_copy(
                src.at[pl.ds(i * CUT, CUT)],
                dst.at[which[1], pl.ds(i * CUT, CUT), pl.ds(0, YM), :],
                sem.at[i],
            )
            for i in range(CUTS)
        ]
        for copy in copies:
            copy.start()
        for copy in copies:
            copy.wait()

    return pl.pallas_call(
        body,
        in_specs=[
            pl.BlockSpec(memory_space=pltpu.SMEM),
            pl.BlockSpec(memory_space=pltpu.VMEM),
            pl.BlockSpec(memory_space=pltpu.HBM),
        ],
        out_specs=pl.BlockSpec(memory_space=pltpu.HBM),
        out_shape=jax.ShapeDtypeStruct((2, LB, MB, NB), BF),
        scratch_shapes=[pltpu.SemaphoreType.DMA((CUTS,))],
        input_output_aliases={2: 0},
        name="put",
        cost_estimate=pl.CostEstimate(flops=0, bytes_accessed=4 * LB * YM * NB, transcendentals=0),
        compiler_params=pltpu.CompilerParams(vmem_limit_bytes=24 * 1024 * 1024),
    )(pick, got, out)


def to_virtual(summed, v_halves):
    def body(s, v, out):
        flat = s[...].astype(F32).reshape(JB * MB, NB).astype(BF)
        out[...] = dot(flat, v[0]).reshape(JB, MB, HALF).astype(BF)

    return call(
        body,
        (2,),
        [whole((JB, MB, NB)), pl.BlockSpec((1, NB, HALF), lambda h: (h, 0, 0))],
        pl.BlockSpec((JB, MB, HALF), lambda h: (h, 0, 0)),
        jax.ShapeDtypeStruct((NROW, MB, HALF), BF),
        (summed, v_halves),
        flops=2 * JB * MB * NB * NV,
    )


def divide(second, coef, coef_t, column, row):
    def body(x, v, vt, c, r, out):
        third = dot(vt[...], x[...])
        amplitude = (third / (c[...] + r[...])).astype(BF)
        out[...] = dot(v[...], amplitude).astype(BF)

    return call(
        body,
        (1,),
        [whole((NB, HALF)), whole((NB, NV)), whole((NV, NB)), whole((NV, 1)), whole((1, HALF))],
        whole((NB, HALF)),
        jax.ShapeDtypeStruct((NB, HALF), BF),
        (second, coef, coef_t, column, row),
        flops=4 * NB * HALF * NV,
    )


def to_basis(back, vt_halves, sizes):
    def body(x, v, *outs):
        flat = [
            x[h * JB : (h + 1) * JB].astype(F32).reshape(JB * MB, HALF).astype(BF) for h in range(2)
        ]
        wide = (dot(flat[0], v[0]) + dot(flat[1], v[1])).reshape(JB, MB, NB)
        lo = 0
        for out, size in zip(outs, sizes):
            out[...] = wide[:, lo : lo + size].astype(BF)
            lo += size

    return call(
        body,
        (1,),
        [whole((NROW, MB, HALF)), whole((2, HALF, NB))],
        [whole((JB, size, NB)) for size in sizes],
        [jax.ShapeDtypeStruct((JB, size, NB), BF) for size in sizes],
        (back, vt_halves),
        flops=2 * JB * MB * NB * NV,
    )


def add(*terms):
    total = terms[0].astype(F32)
    for term in terms[1:]:
        total = total + term.astype(F32)
    return total.astype(BF)


def move(x, step):
    return lax.ppermute(x, "z", [(i, (i + step) % NZ) for i in range(NZ)])


def swap(x):
    return lax.ppermute(x, "ylo", SWAP)


def unrolled(parts):
    return [*parts[NZ - LEAD :], *parts[: NZ - LEAD]]


def chain_sum(parts):
    up, down = parts[3], parts[FAR]
    for n in range(1, FAR + 1):
        if n < FAR:
            up = move(up, 1)
            up = add(up, parts[3 - n]) if n < 3 else up
        down = move(down, -1)
        down = add(down, parts[FAR + n]) if n < FAR else down
    return add(parts[0], up, down)


def tree_sum(parts):
    up = move(parts[3], 1)
    down = move(parts[5], -1)
    far = move(parts[FAR], 2)
    up = add(up, parts[2], far)
    down = add(down, parts[6])
    up = add(move(up, 1), parts[1])
    down = add(move(down, -1), parts[7])
    return add(parts[0], move(up, 1), move(down, -1))


def chain_gather(own):
    slots = [own] + [None] * (NZ - 1)
    up = down = own
    for n in range(1, FAR + 1):
        if n < FAR:
            up = slots[NZ - n] = move(up, 1)
        down = slots[n] = move(down, -1)
    return rolled(slots)


def tree_gather(own):
    up1 = move(own, 1)
    down1 = move(own, -1)
    up2 = move(up1, 1)
    down2 = move(down1, -1)
    up3 = move(up2, 1)
    down3 = move(down2, -1)
    high = move(up2[:JH], 2)
    low = move(down2[JH:], -2)
    return [down3, high, low, up3, up2, up1, own, down1, down2]


def run(slab, coef_virtual, coef_occupied, occ_level, virt_level, orbital_index):
    zi = lax.axis_index("z")
    yi = lax.axis_index("ylo")
    ri = lax.axis_index("row")
    slab = pltpu.with_memory_space_constraint(slab, pltpu.HBM)
    pick = jnp.stack([yi, 1 - yi]).astype(jnp.int32)
    eo = occ_level.astype(F32) / 64.0
    ev = virt_level.astype(F32) / 64.0
    occs = jnp.arange(NO, dtype=jnp.int32)
    chosen = jnp.sum(jnp.where(jnp.arange(2) == yi, orbital_index, 0))
    energy_i = jnp.sum(jnp.where(occs == chosen, eo, 0.0))
    energy_j = jnp.sum(jnp.where(occs == zi * JB + ri % JB, eo, 0.0))
    row = (jnp.where(ri // JB == 0, ev[:HALF], ev[HALF:]) - energy_i - energy_j)[None, :]
    column = ev[:, None]
    coef_t = coef_virtual.T
    v_halves = jnp.stack([coef_virtual[:, :HALF], coef_virtual[:, HALF:]])
    vt_halves = coef_t.reshape(2, HALF, NB)

    raised, coef_o = lax.optimization_barrier((lift(slab, pick), coef_occupied.T))
    swapped = swap(raised)
    k_mine = spread(coef_o, zi * 2 * LB + yi * LB, zi)
    k_other = spread(coef_o, zi * 2 * LB + (1 - yi) * LB, zi)
    head = z_parts(slab, k_mine, pick, YT, ZT, 0, 2)
    tail = z_parts(slab, k_mine, pick, YT, ZT, 2, NZ)
    both = chain_sum(unrolled([*head, *tail]))
    last = add(both[0], swap(both[1]))
    head = y_parts(slab, swapped, k_mine, k_other, pick, 0, YT, 0, 3)
    tail = y_parts(slab, swapped, k_mine, k_other, pick, 0, YT, 3, NZ)
    lead = tree_sum(unrolled([*head, *tail]))
    summed = jnp.concatenate([lead, last], axis=1)

    first = to_virtual(summed, v_halves)
    second = lax.all_to_all(first, "row", 0, 0, tiled=True).reshape(NB, HALF)
    back_one = divide(second, coef_virtual, coef_t, column, row)
    back = lax.all_to_all(back_one.reshape(NROW, MB, HALF), "row", 0, 0, tiled=True)
    wide_y, wide_z = to_basis(back, vt_halves, (YM, ZM))

    kt_mine, kt_other = k_mine.T, k_other.T
    slots = tree_gather(wide_y)
    got = swap(y_send(slots, kt_other, YT))
    out = y_keep(slots, kt_mine, pick, 0, YT)
    both = jnp.stack([wide_z, swap(wide_z)])
    out = z_expand(chain_gather(both), kt_mine, out, pick, YT, ZT)
    return put(got, out, pick)


def solution(mesh):
    fine = Mesh(mesh.devices.reshape(NROW, NZ, 2), ("row", "z", "ylo"))
    slab = P(None, ("z", "ylo"), "row", None)
    return jax.shard_map(
        run, mesh=fine, in_specs=(slab, P(), P(), P(), P(), P()), out_specs=slab, check_vma=False
    )
```

```python
import jax
import jax.numpy as jnp
from jax import lax
from jax.experimental import pallas as pl
from jax.experimental.pallas import tpu as pltpu
from jax.sharding import Mesh, PartitionSpec as P


NB = 640
NO = 64
NV = 576
NROW = 16
NZ = 8
TILE = 8
JB = NO // NZ
LB = NB // 16
MB = NB // NROW
HALF = NV // 2
RW = NO * TILE
CL = LB * TILE
BF = jnp.bfloat16
F32 = jnp.float32
SWAP = [(0, 1), (1, 0)]
YT, ZT = 3, 2
YM, ZM = YT * TILE, ZT * TILE
LEAD = 3
FAR = NZ // 2
JH = JB // 2


def dot(a, b):
    return lax.dot_general(a, b, (((1,), (0,)), ((), ())), preferred_element_type=F32)


def call(body, grid, in_specs, out_specs, out_shape, args, scalars=None, aliases=None, flops=0):
    nbytes = sum(a.size * a.dtype.itemsize for a in args) // 2
    spec = pltpu.PrefetchScalarGridSpec(
        num_scalar_prefetch=0 if scalars is None else 1,
        grid=grid,
        in_specs=in_specs,
        out_specs=out_specs,
    )
    lead = () if scalars is None else (scalars,)
    return pl.pallas_call(
        body,
        grid_spec=spec,
        out_shape=out_shape,
        input_output_aliases=aliases or {},
        cost_estimate=pl.CostEstimate(flops=flops, bytes_accessed=nbytes, transcendentals=0),
        compiler_params=pltpu.CompilerParams(vmem_limit_bytes=24 * 1024 * 1024),
    )(*lead, *args)


def spread(coef_t, base, zi):
    lam = lax.broadcasted_iota(jnp.int32, (NB, CL), 0)
    col = lax.broadcasted_iota(jnp.int32, (NB, CL), 1)
    pick = (lam == base + col // TILE).astype(BF)
    wide = dot(coef_t, pick).astype(BF)
    row = lax.broadcasted_iota(jnp.int32, (RW, NO), 0)
    occ = lax.broadcasted_iota(jnp.int32, (RW, NO), 1)
    block = row // TILE
    want = ((zi + block // JB + LEAD) % NZ) * JB + block % JB
    tall = dot((occ == want).astype(BF), wide)
    row = lax.broadcasted_iota(jnp.int32, (RW, CL), 0)
    col = lax.broadcasted_iota(jnp.int32, (RW, CL), 1)
    return jnp.where(row % TILE == col % TILE, tall, 0.0).astype(BF)


def fold(x):
    return x.astype(F32).reshape(x.shape[0] * x.shape[1], x.shape[2]).astype(BF)


def whole(shape):
    return pl.BlockSpec(shape, lambda *_: (0,) * len(shape))


CUTS = 4
CUT = LB // CUTS
FLOWS = 2
FLOW = LB // FLOWS


def lift(slab, pick):
    def body(which, src, *refs):
        dsts, (hold, came, went) = refs[:FLOWS], refs[FLOWS:]

        def spot(i):
            return pl.ds(i * CUT, CUT)

        takes = [
            pltpu.make_async_copy(
                src.at[which[1], spot(i), pl.ds(0, YM), :], hold.at[spot(i)], came.at[i]
            )
            for i in range(CUTS)
        ]
        gives = [
            pltpu.make_async_copy(
                hold.at[spot(i)], dsts[i * CUT // FLOW].at[pl.ds(i * CUT % FLOW, CUT)], went.at[i]
            )
            for i in range(CUTS)
        ]
        for take in takes:
            take.start()
        for take, give in zip(takes, gives):
            take.wait()
            give.start()
        for give in gives:
            give.wait()

    return pl.pallas_call(
        body,
        in_specs=[pl.BlockSpec(memory_space=pltpu.SMEM), pl.BlockSpec(memory_space=pltpu.HBM)],
        out_specs=[pl.BlockSpec(memory_space=pltpu.HBM)] * FLOWS,
        out_shape=[jax.ShapeDtypeStruct((FLOW, YM, NB), BF)] * FLOWS,
        scratch_shapes=[
            pltpu.VMEM((LB, YM, NB), BF),
            pltpu.SemaphoreType.DMA((CUTS,)),
            pltpu.SemaphoreType.DMA((CUTS,)),
        ],
        name="lift",
        cost_estimate=pl.CostEstimate(flops=0, bytes_accessed=4 * LB * YM * NB, transcendentals=0),
        compiler_params=pltpu.CompilerParams(vmem_limit_bytes=24 * 1024 * 1024),
    )(pick, slab)


def y_parts(slab, swapped, k_mine, k_other, pick, first, tiles, lo, hi):
    rows = slice(lo * JB * TILE, hi * JB * TILE)

    def body(_, here, *refs):
        came, (km, ko), outs = refs[:FLOWS], refs[FLOWS : FLOWS + 2], refs[FLOWS + 2 :]
        part = dot(km[rows], fold(here[0])) + dot(ko[rows], gathered([c[...] for c in came]))
        part = part.reshape(hi - lo, JB, TILE, NB)
        for k, out in enumerate(outs):
            out[...] = part[k].astype(BF)

    return call(
        body,
        (tiles,),
        [
            pl.BlockSpec((1, LB, TILE, NB), lambda t, s: (s[0], 0, first + t, 0)),
            *[pl.BlockSpec((FLOW, TILE, NB), lambda t, s: (0, t, 0))] * FLOWS,
            whole((RW, CL)),
            whole((RW, CL)),
        ],
        [pl.BlockSpec((JB, TILE, NB), lambda t, s: (0, t, 0))] * (hi - lo),
        [jax.ShapeDtypeStruct((JB, tiles * TILE, NB), BF)] * (hi - lo),
        (slab, *swapped, k_mine, k_other),
        pick,
        flops=4 * tiles * (hi - lo) * JB * TILE * CL * NB,
    )


def z_parts(slab, k_mine, pick, first, tiles, lo, hi, after=()):
    rows = slice(lo * JB * TILE, hi * JB * TILE)

    def body(_, here, km, *refs):
        outs = refs[len(after) :]
        part = dot(km[rows], fold(here[0])).reshape(hi - lo, JB, TILE, NB)
        for k, out in enumerate(outs):
            out[0] = part[k].astype(BF)

    return call(
        body,
        (2, tiles),
        [
            pl.BlockSpec((1, LB, TILE, NB), lambda o, t, s: (s[o], 0, first + t, 0)),
            whole((RW, CL)),
            *[pl.BlockSpec(memory_space=pl.ANY)] * len(after),
        ],
        [pl.BlockSpec((1, JB, TILE, NB), lambda o, t, s: (o, 0, t, 0))] * (hi - lo),
        [jax.ShapeDtypeStruct((2, JB, tiles * TILE, NB), BF)] * (hi - lo),
        (slab, k_mine, *after),
        pick,
        flops=4 * tiles * (hi - lo) * JB * TILE * CL * NB,
    )


def gathered(slots):
    return jnp.concatenate([fold(s) for s in slots], axis=0)


def rolled(slots):
    return [*slots[LEAD:], *slots[:LEAD]]


def y_send(slots, kt_other, tiles):
    def body(*refs):
        slot_refs, (ko, *sends) = refs[: len(slots)], refs[len(slots) :]
        stack = gathered([s[...] for s in slot_refs])
        block = dot(ko[...], stack).reshape(LB, TILE, NB)
        for i, send in enumerate(sends):
            send[...] = block[i * FLOW : (i + 1) * FLOW].astype(BF)

    return call(
        body,
        (tiles,),
        [pl.BlockSpec((s.shape[0], TILE, NB), lambda t: (0, t, 0)) for s in slots]
        + [whole((CL, RW))],
        [pl.BlockSpec((FLOW, TILE, NB), lambda t: (0, t, 0))] * FLOWS,
        [jax.ShapeDtypeStruct((FLOW, tiles * TILE, NB), BF)] * FLOWS,
        (*slots, kt_other),
        flops=2 * tiles * RW * CL * NB,
    )


def y_keep(slots, kt_mine, pick, first, tiles):
    def body(_, *refs):
        slot_refs, (km, kept) = refs[: len(slots)], refs[len(slots) :]
        stack = gathered([s[...] for s in slot_refs])
        kept[0] = dot(km[...], stack).reshape(LB, TILE, NB).astype(BF)

    return call(
        body,
        (tiles,),
        [pl.BlockSpec((s.shape[0], TILE, NB), lambda t, s: (0, t, 0)) for s in slots]
        + [whole((CL, RW))],
        pl.BlockSpec((1, LB, TILE, NB), lambda t, s: (s[0], 0, first + t, 0)),
        jax.ShapeDtypeStruct((2, LB, MB, NB), BF),
        (*slots, kt_mine),
        pick,
        flops=2 * tiles * RW * CL * NB,
    )


def z_expand(slots, kt_mine, out, pick, first, tiles):
    def body(_, *refs):
        slot_refs, km, kept = refs[:NZ], refs[NZ], refs[NZ + 2]
        stack = gathered([s[0] for s in slot_refs])
        kept[0] = dot(km[...], stack).reshape(LB, TILE, NB).astype(BF)

    return call(
        body,
        (2, tiles),
        [pl.BlockSpec((1, JB, TILE, NB), lambda o, t, s: (o, 0, t, 0))] * NZ
        + [whole((CL, RW)), pl.BlockSpec(memory_space=pl.ANY)],
        pl.BlockSpec((1, LB, TILE, NB), lambda o, t, s: (s[o], 0, first + t, 0)),
        jax.ShapeDtypeStruct((2, LB, MB, NB), BF),
        (*slots, kt_mine, out),
        pick,
        {NZ + 2: 0},
        flops=4 * tiles * RW * CL * NB,
    )


def put(got, out, pick):
    def body(which, *refs):
        srcs, (_, dst, sem) = refs[:FLOWS], refs[FLOWS:]
        copies = [
            pltpu.make_async_copy(
                srcs[i * CUT // FLOW].at[pl.ds(i * CUT % FLOW, CUT)],
                dst.at[which[1], pl.ds(i * CUT, CUT), pl.ds(0, YM), :],
                sem.at[i],
            )
            for i in range(CUTS)
        ]
        for copy in copies:
            copy.start()
        for copy in copies:
            copy.wait()

    return pl.pallas_call(
        body,
        in_specs=[
            pl.BlockSpec(memory_space=pltpu.SMEM),
            *[pl.BlockSpec(memory_space=pl.ANY)] * FLOWS,
            pl.BlockSpec(memory_space=pltpu.HBM),
        ],
        out_specs=pl.BlockSpec(memory_space=pltpu.HBM),
        out_shape=jax.ShapeDtypeStruct((2, LB, MB, NB), BF),
        scratch_shapes=[pltpu.SemaphoreType.DMA((CUTS,))],
        input_output_aliases={1 + FLOWS: 0},
        name="put",
        cost_estimate=pl.CostEstimate(flops=0, bytes_accessed=4 * LB * YM * NB, transcendentals=0),
        compiler_params=pltpu.CompilerParams(vmem_limit_bytes=24 * 1024 * 1024),
    )(pick, *got, out)


def to_virtual(summed, v_halves):
    def body(s, v, out):
        flat = s[...].astype(F32).reshape(JB * MB, NB).astype(BF)
        out[...] = dot(flat, v[0]).reshape(JB, MB, HALF).astype(BF)

    return call(
        body,
        (2,),
        [whole((JB, MB, NB)), pl.BlockSpec((1, NB, HALF), lambda h: (h, 0, 0))],
        pl.BlockSpec((JB, MB, HALF), lambda h: (h, 0, 0)),
        jax.ShapeDtypeStruct((NROW, MB, HALF), BF),
        (summed, v_halves),
        flops=2 * JB * MB * NB * NV,
    )


def divide(second, coef, coef_t, column, row):
    def body(x, v, vt, c, r, out):
        third = dot(vt[...], x[...])
        amplitude = (third / (c[...] + r[...])).astype(BF)
        out[...] = dot(v[...], amplitude).astype(BF)

    return call(
        body,
        (1,),
        [whole((NB, HALF)), whole((NB, NV)), whole((NV, NB)), whole((NV, 1)), whole((1, HALF))],
        whole((NB, HALF)),
        jax.ShapeDtypeStruct((NB, HALF), BF),
        (second, coef, coef_t, column, row),
        flops=4 * NB * HALF * NV,
    )


def to_basis(back, vt_halves, sizes):
    def body(x, v, *outs):
        flat = [
            x[h * JB : (h + 1) * JB].astype(F32).reshape(JB * MB, HALF).astype(BF) for h in range(2)
        ]
        wide = (dot(flat[0], v[0]) + dot(flat[1], v[1])).reshape(JB, MB, NB)
        lo = 0
        for out, size in zip(outs, sizes):
            out[...] = wide[:, lo : lo + size].astype(BF)
            lo += size

    return call(
        body,
        (1,),
        [whole((NROW, MB, HALF)), whole((2, HALF, NB))],
        [whole((JB, size, NB)) for size in sizes],
        [jax.ShapeDtypeStruct((JB, size, NB), BF) for size in sizes],
        (back, vt_halves),
        flops=2 * JB * MB * NB * NV,
    )


def add(*terms):
    total = terms[0].astype(F32)
    for term in terms[1:]:
        total = total + term.astype(F32)
    return total.astype(BF)


def move(x, step):
    return lax.ppermute(x, "z", [(i, (i + step) % NZ) for i in range(NZ)])


def swap(x):
    return lax.ppermute(x, "ylo", SWAP)


def unrolled(parts):
    return [*parts[NZ - LEAD :], *parts[: NZ - LEAD]]


def chain_sum(parts):
    up, down = parts[3], parts[FAR]
    for n in range(1, FAR + 1):
        if n < FAR:
            up = move(up, 1)
            up = add(up, parts[3 - n]) if n < 3 else up
        down = move(down, -1)
        down = add(down, parts[FAR + n]) if n < FAR else down
    return add(parts[0], up, down)


def tree_sum(parts):
    up = move(parts[3], 1)
    down = move(parts[5], -1)
    far = move(parts[FAR], 2)
    up = add(up, parts[2], far)
    down = add(down, parts[6])
    up = add(move(up, 1), parts[1])
    down = add(move(down, -1), parts[7])
    return add(parts[0], move(up, 1), move(down, -1))


def chain_gather(own):
    slots = [own] + [None] * (NZ - 1)
    up = down = own
    for n in range(1, FAR + 1):
        if n < FAR:
            up = slots[NZ - n] = move(up, 1)
        down = slots[n] = move(down, -1)
    return rolled(slots)


def tree_gather(own):
    up1 = move(own, 1)
    down1 = move(own, -1)
    up2 = move(up1, 1)
    down2 = move(down1, -1)
    up3 = move(up2, 1)
    down3 = move(down2, -1)
    high = move(up2[:JH], 2)
    low = move(down2[JH:], -2)
    return [down3, high, low, up3, up2, up1, own, down1, down2]


def run(slab, coef_virtual, coef_occupied, occ_level, virt_level, orbital_index):
    zi = lax.axis_index("z")
    yi = lax.axis_index("ylo")
    ri = lax.axis_index("row")
    slab = pltpu.with_memory_space_constraint(slab, pltpu.HBM)
    pick = jnp.stack([yi, 1 - yi]).astype(jnp.int32)
    eo = occ_level.astype(F32) / 64.0
    ev = virt_level.astype(F32) / 64.0
    occs = jnp.arange(NO, dtype=jnp.int32)
    chosen = jnp.sum(jnp.where(jnp.arange(2) == yi, orbital_index, 0))
    energy_i = jnp.sum(jnp.where(occs == chosen, eo, 0.0))
    energy_j = jnp.sum(jnp.where(occs == zi * JB + ri % JB, eo, 0.0))
    row = (jnp.where(ri // JB == 0, ev[:HALF], ev[HALF:]) - energy_i - energy_j)[None, :]
    column = ev[:, None]
    coef_t = coef_virtual.T
    v_halves = jnp.stack([coef_virtual[:, :HALF], coef_virtual[:, HALF:]])
    vt_halves = coef_t.reshape(2, HALF, NB)

    raised, coef_o = lax.optimization_barrier((lift(slab, pick), coef_occupied.T))
    swapped = [swap(r) for r in raised]
    k_mine = spread(coef_o, zi * 2 * LB + yi * LB, zi)
    head = z_parts(slab, k_mine, pick, YT, ZT, 0, 2)
    coef_o, _ = lax.optimization_barrier((coef_o, head[0]))
    k_other = spread(coef_o, zi * 2 * LB + (1 - yi) * LB, zi)
    tail = z_parts(slab, k_mine, pick, YT, ZT, 2, NZ, (k_other,))
    both = chain_sum(unrolled([*head, *tail]))
    last = add(both[0], swap(both[1]))
    head = y_parts(slab, swapped, k_mine, k_other, pick, 0, YT, 0, 3)
    tail = y_parts(slab, swapped, k_mine, k_other, pick, 0, YT, 3, NZ)
    lead = tree_sum(unrolled([*head, *tail]))
    summed = jnp.concatenate([lead, last], axis=1)

    first = to_virtual(summed, v_halves)
    second = lax.all_to_all(first, "row", 0, 0, tiled=True).reshape(NB, HALF)
    back_one = divide(second, coef_virtual, coef_t, column, row)
    back = lax.all_to_all(back_one.reshape(NROW, MB, HALF), "row", 0, 0, tiled=True)
    wide_y, wide_z = to_basis(back, vt_halves, (YM, ZM))

    kt_mine, kt_other = k_mine.T, k_other.T
    slots = tree_gather(wide_y)
    got = [swap(b) for b in y_send(slots, kt_other, YT)]
    out = y_keep(slots, kt_mine, pick, 0, YT)
    both = jnp.stack([wide_z, swap(wide_z)])
    out = z_expand(chain_gather(both), kt_mine, out, pick, YT, ZT)
    return put(got, out, pick)


def solution(mesh):
    fine = Mesh(mesh.devices.reshape(NROW, NZ, 2), ("row", "z", "ylo"))
    slab = P(None, ("z", "ylo"), "row", None)
    return jax.shard_map(
        run, mesh=fine, in_specs=(slab, P(), P(), P(), P(), P()), out_specs=slab, check_vma=False
    )
```

```python
import jax
import jax.numpy as jnp
from jax import lax
from jax.experimental import pallas as pl
from jax.experimental.pallas import tpu as pltpu
from jax.sharding import Mesh, PartitionSpec as P


NB = 640
NO = 64
NV = 576
NROW = 16
NZ = 8
TILE = 8
JB = NO // NZ
LB = NB // 16
MB = NB // NROW
HALF = NV // 2
RW = NO * TILE
CL = LB * TILE
BF = jnp.bfloat16
F32 = jnp.float32
SWAP = [(0, 1), (1, 0)]
YT, ZT = 3, 2
YM, ZM = YT * TILE, ZT * TILE
LEAD = 3
FAR = NZ // 2
JH = 6


def dot(a, b):
    return lax.dot_general(a, b, (((1,), (0,)), ((), ())), preferred_element_type=F32)


def call(body, grid, in_specs, out_specs, out_shape, args, scalars=None, aliases=None, flops=0):
    nbytes = sum(a.size * a.dtype.itemsize for a in args) // 2
    spec = pltpu.PrefetchScalarGridSpec(
        num_scalar_prefetch=0 if scalars is None else 1,
        grid=grid,
        in_specs=in_specs,
        out_specs=out_specs,
    )
    lead = () if scalars is None else (scalars,)
    return pl.pallas_call(
        body,
        grid_spec=spec,
        out_shape=out_shape,
        input_output_aliases=aliases or {},
        cost_estimate=pl.CostEstimate(flops=flops, bytes_accessed=nbytes, transcendentals=0),
        compiler_params=pltpu.CompilerParams(vmem_limit_bytes=24 * 1024 * 1024),
    )(*lead, *args)


def spread(coef_t, base, zi):
    lam = lax.broadcasted_iota(jnp.int32, (NB, CL), 0)
    col = lax.broadcasted_iota(jnp.int32, (NB, CL), 1)
    pick = (lam == base + col // TILE).astype(BF)
    wide = dot(coef_t, pick).astype(BF)
    row = lax.broadcasted_iota(jnp.int32, (RW, NO), 0)
    occ = lax.broadcasted_iota(jnp.int32, (RW, NO), 1)
    block = row // TILE
    want = ((zi + block // JB + LEAD) % NZ) * JB + block % JB
    tall = dot((occ == want).astype(BF), wide)
    row = lax.broadcasted_iota(jnp.int32, (RW, CL), 0)
    col = lax.broadcasted_iota(jnp.int32, (RW, CL), 1)
    return jnp.where(row % TILE == col % TILE, tall, 0.0).astype(BF)


def fold(x):
    return x.astype(F32).reshape(x.shape[0] * x.shape[1], x.shape[2]).astype(BF)


def whole(shape):
    return pl.BlockSpec(shape, lambda *_: (0,) * len(shape))


CUTS = 5
CUT = LB // CUTS


def lift(slab):
    def body(src, dst, hold, came, went):
        there = 1 - lax.axis_index("ylo")

        def spot(i):
            return pl.ds(i * CUT, CUT)

        takes = [
            pltpu.make_async_copy(
                src.at[there, spot(i), pl.ds(0, YM), :], hold.at[spot(i)], came.at[i]
            )
            for i in range(CUTS)
        ]
        gives = [
            pltpu.make_async_copy(hold.at[spot(i)], dst.at[spot(i)], went.at[i])
            for i in range(CUTS)
        ]
        for take in takes:
            take.start()
        for take, give in zip(takes, gives):
            take.wait()
            give.start()
        for give in gives:
            give.wait()

    return pl.pallas_call(
        body,
        in_specs=[pl.BlockSpec(memory_space=pltpu.HBM)],
        out_specs=pl.BlockSpec(memory_space=pltpu.HBM),
        out_shape=jax.ShapeDtypeStruct((LB, YM, NB), BF),
        scratch_shapes=[
            pltpu.VMEM((LB, YM, NB), BF),
            pltpu.SemaphoreType.DMA((CUTS,)),
            pltpu.SemaphoreType.DMA((CUTS,)),
        ],
        name="lift",
        cost_estimate=pl.CostEstimate(flops=0, bytes_accessed=4 * LB * YM * NB, transcendentals=0),
        compiler_params=pltpu.CompilerParams(vmem_limit_bytes=24 * 1024 * 1024),
    )(slab)


def y_parts(slab, swapped, k_mine, k_other, pick, first, tiles, lo, hi):
    rows = slice(lo * JB * TILE, hi * JB * TILE)

    def body(_, here, came, km, ko, *outs):
        part = dot(km[rows], fold(here[0])) + dot(ko[rows], fold(came[...]))
        part = part.reshape(hi - lo, JB, TILE, NB)
        for k, out in enumerate(outs):
            out[...] = part[k].astype(BF)

    return call(
        body,
        (tiles,),
        [
            pl.BlockSpec((1, LB, TILE, NB), lambda t, s: (s[0], 0, first + t, 0)),
            pl.BlockSpec((LB, TILE, NB), lambda t, s: (0, t, 0)),
            whole((RW, CL)),
            whole((RW, CL)),
        ],
        [pl.BlockSpec((JB, TILE, NB), lambda t, s: (0, t, 0))] * (hi - lo),
        [jax.ShapeDtypeStruct((JB, tiles * TILE, NB), BF)] * (hi - lo),
        (slab, swapped, k_mine, k_other),
        pick,
        flops=4 * tiles * (hi - lo) * JB * TILE * CL * NB,
    )


def beside(take, tiles):
    return jnp.concatenate([take(slice(t * TILE, (t + 1) * TILE)) for t in range(tiles)], axis=1)


def z_parts(slab, k_mine, pick, first, tiles, lo, hi):
    rows = slice(lo * JB * TILE, hi * JB * TILE)

    def body(_, here, km, *outs):
        wide = dot(km[rows], beside(lambda spot: fold(here[0, :, spot]), tiles))
        for t in range(tiles):
            part = wide[:, t * NB : (t + 1) * NB].reshape(hi - lo, JB, TILE, NB)
            for k, out in enumerate(outs):
                out[0, :, t * TILE : (t + 1) * TILE] = part[k].astype(BF)

    return call(
        body,
        (2,),
        [
            pl.BlockSpec(
                tuple(pl.Element(n) for n in (1, LB, tiles * TILE, NB)),
                lambda o, s: (s[o], 0, first * TILE, 0),
            ),
            whole((RW, CL)),
        ],
        [pl.BlockSpec((1, JB, tiles * TILE, NB), lambda o, s: (o, 0, 0, 0))] * (hi - lo),
        [jax.ShapeDtypeStruct((2, JB, tiles * TILE, NB), BF)] * (hi - lo),
        (slab, k_mine),
        pick,
        flops=4 * tiles * (hi - lo) * JB * TILE * CL * NB,
    )


def gathered(slots):
    return jnp.concatenate([fold(s) for s in slots], axis=0)


def rolled(slots):
    return [*slots[LEAD:], *slots[:LEAD]]


def y_send(slots, kt_other, tiles):
    def body(*refs):
        slot_refs, (ko, send) = refs[: len(slots)], refs[len(slots) :]
        stack = gathered([s[...] for s in slot_refs])
        send[...] = dot(ko[...], stack).reshape(LB, TILE, NB).astype(BF)

    return call(
        body,
        (tiles,),
        [pl.BlockSpec((s.shape[0], TILE, NB), lambda t: (0, t, 0)) for s in slots]
        + [whole((CL, RW))],
        pl.BlockSpec((LB, TILE, NB), lambda t: (0, t, 0)),
        jax.ShapeDtypeStruct((LB, tiles * TILE, NB), BF),
        (*slots, kt_other),
        flops=2 * tiles * RW * CL * NB,
    )


def y_keep(slots, kt_mine, pick, first, tiles):
    def body(_, *refs):
        slot_refs, (km, kept) = refs[: len(slots)], refs[len(slots) :]
        stack = gathered([s[...] for s in slot_refs])
        kept[0] = dot(km[...], stack).reshape(LB, TILE, NB).astype(BF)

    return call(
        body,
        (tiles,),
        [pl.BlockSpec((s.shape[0], TILE, NB), lambda t, s: (0, t, 0)) for s in slots]
        + [whole((CL, RW))],
        pl.BlockSpec((1, LB, TILE, NB), lambda t, s: (s[0], 0, first + t, 0)),
        jax.ShapeDtypeStruct((2, LB, MB, NB), BF),
        (*slots, kt_mine),
        pick,
        flops=2 * tiles * RW * CL * NB,
    )


def z_expand(slots, kt_mine, out, pick, first, tiles):
    def body(_, *refs):
        slot_refs, km, kept = refs[:NZ], refs[NZ], refs[NZ + 2]
        wide = dot(
            km[...], beside(lambda spot: gathered([s[0, :, spot] for s in slot_refs]), tiles)
        )
        for t in range(tiles):
            part = wide[:, t * NB : (t + 1) * NB].reshape(LB, TILE, NB)
            kept[0, :, t * TILE : (t + 1) * TILE] = part.astype(BF)

    return call(
        body,
        (2,),
        [pl.BlockSpec((1, JB, tiles * TILE, NB), lambda o, s: (o, 0, 0, 0))] * NZ
        + [whole((CL, RW)), pl.BlockSpec(memory_space=pl.ANY)],
        pl.BlockSpec(
            tuple(pl.Element(n) for n in (1, LB, tiles * TILE, NB)),
            lambda o, s: (s[o], 0, first * TILE, 0),
        ),
        jax.ShapeDtypeStruct((2, LB, MB, NB), BF),
        (*slots, kt_mine, out),
        pick,
        {NZ + 2: 0},
        flops=4 * tiles * RW * CL * NB,
    )


def put(got, out):
    def body(src, _, dst, sem):
        there = 1 - lax.axis_index("ylo")
        copies = [
            pltpu.make_async_copy(
                src.at[pl.ds(i * CUT, CUT)],
                dst.at[there, pl.ds(i * CUT, CUT), pl.ds(0, YM), :],
                sem.at[i],
            )
            for i in range(CUTS)
        ]
        for copy in copies:
            copy.start()
        for copy in copies:
            copy.wait()

    return pl.pallas_call(
        body,
        in_specs=[
            pl.BlockSpec(memory_space=pl.ANY),
            pl.BlockSpec(memory_space=pltpu.HBM),
        ],
        out_specs=pl.BlockSpec(memory_space=pltpu.HBM),
        out_shape=jax.ShapeDtypeStruct((2, LB, MB, NB), BF),
        scratch_shapes=[pltpu.SemaphoreType.DMA((CUTS,))],
        input_output_aliases={1: 0},
        name="put",
        cost_estimate=pl.CostEstimate(flops=0, bytes_accessed=4 * LB * YM * NB, transcendentals=0),
        compiler_params=pltpu.CompilerParams(vmem_limit_bytes=24 * 1024 * 1024),
    )(got, out)


def to_virtual(summed, v_halves):
    def body(s, v, out):
        flat = s[...].astype(F32).reshape(JB * MB, NB).astype(BF)
        out[...] = dot(flat, v[0]).reshape(JB, MB, HALF).astype(BF)

    return call(
        body,
        (2,),
        [whole((JB, MB, NB)), pl.BlockSpec((1, NB, HALF), lambda h: (h, 0, 0))],
        pl.BlockSpec((JB, MB, HALF), lambda h: (h, 0, 0)),
        jax.ShapeDtypeStruct((NROW, MB, HALF), BF),
        (summed, v_halves),
        flops=2 * JB * MB * NB * NV,
    )


def divide(second, coef, coef_t, column, row):
    def body(x, v, vt, c, r, out):
        third = dot(vt[...], x[...])
        amplitude = (third / (c[...] + r[...])).astype(BF)
        out[...] = dot(v[...], amplitude).astype(BF)

    return call(
        body,
        (1,),
        [whole((NB, HALF)), whole((NB, NV)), whole((NV, NB)), whole((NV, 1)), whole((1, HALF))],
        whole((NB, HALF)),
        jax.ShapeDtypeStruct((NB, HALF), BF),
        (second, coef, coef_t, column, row),
        flops=4 * NB * HALF * NV,
    )


def to_basis(back, vt_halves, sizes):
    def body(x, v, *outs):
        flat = [
            x[h * JB : (h + 1) * JB].astype(F32).reshape(JB * MB, HALF).astype(BF) for h in range(2)
        ]
        wide = (dot(flat[0], v[0]) + dot(flat[1], v[1])).reshape(JB, MB, NB)
        lo = 0
        for out, size in zip(outs, sizes):
            out[...] = wide[:, lo : lo + size].astype(BF)
            lo += size

    return call(
        body,
        (1,),
        [whole((NROW, MB, HALF)), whole((2, HALF, NB))],
        [whole((JB, size, NB)) for size in sizes],
        [jax.ShapeDtypeStruct((JB, size, NB), BF) for size in sizes],
        (back, vt_halves),
        flops=2 * JB * MB * NB * NV,
    )


def add(*terms):
    total = terms[0].astype(F32)
    for term in terms[1:]:
        total = total + term.astype(F32)
    return total.astype(BF)


def move(x, step):
    return lax.ppermute(x, "z", [(i, (i + step) % NZ) for i in range(NZ)])


def swap(x):
    return lax.ppermute(x, "ylo", SWAP)


def unrolled(parts):
    return [*parts[NZ - LEAD :], *parts[: NZ - LEAD]]


def chain_sum(parts):
    up, down = parts[3], parts[FAR]
    for n in range(1, FAR + 1):
        if n < FAR:
            up = move(up, 1)
            up = add(up, parts[3 - n]) if n < 3 else up
        down = move(down, -1)
        down = add(down, parts[FAR + n]) if n < FAR else down
    return add(parts[0], up, down)


def tree_sum(parts):
    up = move(parts[3], 1)
    down = move(parts[5], -1)
    far = move(parts[FAR], 2)
    up = add(up, parts[2], far)
    down = add(down, parts[6])
    up = add(move(up, 1), parts[1])
    down = add(move(down, -1), parts[7])
    return add(parts[0], move(up, 1), move(down, -1))


def chain_gather(own):
    slots = [own] + [None] * (NZ - 1)
    up = down = own
    for n in range(1, FAR + 1):
        if n < FAR:
            up = slots[NZ - n] = move(up, 1)
        down = slots[n] = move(down, -1)
    return rolled(slots)


def tree_gather(own):
    up1 = move(own, 1)
    down1 = move(own, -1)
    up2 = move(up1, 1)
    down2 = move(down1, -1)
    up3 = move(up2, 1)
    down3 = move(down2, -1)
    high = move(up2[:JH], 2)
    low = move(down2[JH:], -2)
    return [down3, high, low, up3, up2, up1, own, down1, down2]


def run(slab, coef_virtual, coef_occupied, occ_level, virt_level, orbital_index):
    zi = lax.axis_index("z")
    yi = lax.axis_index("ylo")
    ri = lax.axis_index("row")
    slab = pltpu.with_memory_space_constraint(slab, pltpu.HBM)
    pick = jnp.stack([yi, 1 - yi]).astype(jnp.int32)
    eo = occ_level.astype(F32) / 64.0
    ev = virt_level.astype(F32) / 64.0
    occs = jnp.arange(NO, dtype=jnp.int32)
    chosen = jnp.sum(jnp.where(jnp.arange(2) == yi, orbital_index, 0))
    energy_i = jnp.sum(jnp.where(occs == chosen, eo, 0.0))
    energy_j = jnp.sum(jnp.where(occs == zi * JB + ri % JB, eo, 0.0))
    row = (jnp.where(ri // JB == 0, ev[:HALF], ev[HALF:]) - energy_i - energy_j)[None, :]
    column = ev[:, None]
    coef_t = coef_virtual.T
    v_halves = jnp.stack([coef_virtual[:, :HALF], coef_virtual[:, HALF:]])
    vt_halves = coef_t.reshape(2, HALF, NB)

    raised, coef_o = lax.optimization_barrier((lift(slab), coef_occupied.T))
    swapped = swap(raised)
    k_mine = spread(coef_o, zi * 2 * LB + yi * LB, zi)
    k_other = spread(coef_o, zi * 2 * LB + (1 - yi) * LB, zi)
    head = z_parts(slab, k_mine, pick, YT, ZT, 0, 2)
    tail = z_parts(slab, k_mine, pick, YT, ZT, 2, NZ)
    both = chain_sum(unrolled([*head, *tail]))
    last = add(both[0], swap(both[1]))
    head = y_parts(slab, swapped, k_mine, k_other, pick, 0, YT, 0, 3)
    tail = y_parts(slab, swapped, k_mine, k_other, pick, 0, YT, 3, NZ)
    lead = tree_sum(unrolled([*head, *tail]))
    summed = jnp.concatenate([lead, last], axis=1)

    first = to_virtual(summed, v_halves)
    second = lax.all_to_all(first, "row", 0, 0, tiled=True).reshape(NB, HALF)
    back_one = divide(second, coef_virtual, coef_t, column, row)
    back = lax.all_to_all(back_one.reshape(NROW, MB, HALF), "row", 0, 0, tiled=True)
    wide_y, wide_z = to_basis(back, vt_halves, (YM, ZM))

    kt_mine, kt_other = k_mine.T, k_other.T
    slots = tree_gather(wide_y)
    got = swap(y_send(slots, kt_other, YT))
    out = y_keep(slots, kt_mine, pick, 0, YT)
    both = jnp.stack([wide_z, swap(wide_z)])
    out = z_expand(chain_gather(both), kt_mine, out, pick, YT, ZT)
    return put(got, out)


def solution(mesh):
    fine = Mesh(mesh.devices.reshape(NROW, NZ, 2), ("row", "z", "ylo"))
    slab = P(None, ("z", "ylo"), "row", None)
    return jax.shard_map(
        run, mesh=fine, in_specs=(slab, P(), P(), P(), P(), P()), out_specs=slab, check_vma=False
    )
```

```python
import jax
import jax.numpy as jnp
from jax import lax
from jax.experimental import pallas as pl
from jax.experimental.pallas import tpu as pltpu
from jax.sharding import Mesh, PartitionSpec as P


NB = 640
NO = 64
NV = 576
NROW = 16
NZ = 8
TILE = 8
JB = NO // NZ
LB = NB // 16
MB = NB // NROW
HALF = NV // 2
RW = NO * TILE
CL = LB * TILE
BF = jnp.bfloat16
F32 = jnp.float32
SWAP = [(0, 1), (1, 0)]
YT, ZT = 3, 2
YM, ZM = YT * TILE, ZT * TILE
LEAD = 3
FAR = NZ // 2
JH = JB // 2


def dot(a, b):
    return lax.dot_general(a, b, (((1,), (0,)), ((), ())), preferred_element_type=F32)


def call(body, grid, in_specs, out_specs, out_shape, args, scalars=None, aliases=None, flops=0):
    nbytes = sum(a.size * a.dtype.itemsize for a in args) // 2
    spec = pltpu.PrefetchScalarGridSpec(
        num_scalar_prefetch=0 if scalars is None else 1,
        grid=grid,
        in_specs=in_specs,
        out_specs=out_specs,
    )
    lead = () if scalars is None else (scalars,)
    return pl.pallas_call(
        body,
        grid_spec=spec,
        out_shape=out_shape,
        input_output_aliases=aliases or {},
        cost_estimate=pl.CostEstimate(flops=flops, bytes_accessed=nbytes, transcendentals=0),
        compiler_params=pltpu.CompilerParams(vmem_limit_bytes=24 * 1024 * 1024),
    )(*lead, *args)


def spread(coef_t, base, zi):
    lam = lax.broadcasted_iota(jnp.int32, (NB, CL), 0)
    col = lax.broadcasted_iota(jnp.int32, (NB, CL), 1)
    pick = (lam == base + col // TILE).astype(BF)
    wide = dot(coef_t, pick).astype(BF)
    row = lax.broadcasted_iota(jnp.int32, (RW, NO), 0)
    occ = lax.broadcasted_iota(jnp.int32, (RW, NO), 1)
    block = row // TILE
    want = ((zi + block // JB + LEAD) % NZ) * JB + block % JB
    tall = dot((occ == want).astype(BF), wide)
    row = lax.broadcasted_iota(jnp.int32, (RW, CL), 0)
    col = lax.broadcasted_iota(jnp.int32, (RW, CL), 1)
    return jnp.where(row % TILE == col % TILE, tall, 0.0).astype(BF)


def fold(x):
    return x.astype(F32).reshape(x.shape[0] * x.shape[1], x.shape[2]).astype(BF)


def whole(shape):
    return pl.BlockSpec(shape, lambda *_: (0,) * len(shape))


CUTS = 5
CUT = LB // CUTS


def lift(slab):
    def body(src, dst, hold, came, went):
        there = 1 - lax.axis_index("ylo")

        def spot(i):
            return pl.ds(i * CUT, CUT)

        takes = [
            pltpu.make_async_copy(
                src.at[there, spot(i), pl.ds(0, YM), :], hold.at[spot(i)], came.at[i]
            )
            for i in range(CUTS)
        ]
        gives = [
            pltpu.make_async_copy(hold.at[spot(i)], dst.at[spot(i)], went.at[i])
            for i in range(CUTS)
        ]
        for take in takes:
            take.start()
        for take, give in zip(takes, gives):
            take.wait()
            give.start()
        for give in gives:
            give.wait()

    return pl.pallas_call(
        body,
        in_specs=[pl.BlockSpec(memory_space=pltpu.HBM)],
        out_specs=pl.BlockSpec(memory_space=pltpu.HBM),
        out_shape=jax.ShapeDtypeStruct((LB, YM, NB), BF),
        scratch_shapes=[
            pltpu.VMEM((LB, YM, NB), BF),
            pltpu.SemaphoreType.DMA((CUTS,)),
            pltpu.SemaphoreType.DMA((CUTS,)),
        ],
        name="lift",
        cost_estimate=pl.CostEstimate(flops=0, bytes_accessed=4 * LB * YM * NB, transcendentals=0),
        compiler_params=pltpu.CompilerParams(vmem_limit_bytes=24 * 1024 * 1024),
    )(slab)


def y_parts(slab, swapped, k_mine, k_other, pick, first, tiles, lo, hi):
    rows = slice(lo * JB * TILE, hi * JB * TILE)

    def body(_, here, came, km, ko, *outs):
        part = dot(km[rows], fold(here[0])) + dot(ko[rows], fold(came[...]))
        part = part.reshape(hi - lo, JB, TILE, NB)
        for k, out in enumerate(outs):
            out[...] = part[k].astype(BF)

    return call(
        body,
        (tiles,),
        [
            pl.BlockSpec((1, LB, TILE, NB), lambda t, s: (s[0], 0, first + t, 0)),
            pl.BlockSpec((LB, TILE, NB), lambda t, s: (0, t, 0)),
            whole((RW, CL)),
            whole((RW, CL)),
        ],
        [pl.BlockSpec((JB, TILE, NB), lambda t, s: (0, t, 0))] * (hi - lo),
        [jax.ShapeDtypeStruct((JB, tiles * TILE, NB), BF)] * (hi - lo),
        (slab, swapped, k_mine, k_other),
        pick,
        flops=4 * tiles * (hi - lo) * JB * TILE * CL * NB,
    )


def beside(take, tiles):
    return jnp.concatenate([take(slice(t * TILE, (t + 1) * TILE)) for t in range(tiles)], axis=1)


def z_parts(slab, k_mine, pick, first, tiles, lo, hi):
    rows = slice(lo * JB * TILE, hi * JB * TILE)

    def body(_, here, km, *outs):
        wide = dot(km[rows], beside(lambda spot: fold(here[0, :, spot]), tiles))
        for t in range(tiles):
            part = wide[:, t * NB : (t + 1) * NB].reshape(hi - lo, JB, TILE, NB)
            for k, out in enumerate(outs):
                out[0, :, t * TILE : (t + 1) * TILE] = part[k].astype(BF)

    return call(
        body,
        (2,),
        [
            pl.BlockSpec(
                tuple(pl.Element(n) for n in (1, LB, tiles * TILE, NB)),
                lambda o, s: (s[o], 0, first * TILE, 0),
            ),
            whole((RW, CL)),
        ],
        [pl.BlockSpec((1, JB, tiles * TILE, NB), lambda o, s: (o, 0, 0, 0))] * (hi - lo),
        [jax.ShapeDtypeStruct((2, JB, tiles * TILE, NB), BF)] * (hi - lo),
        (slab, k_mine),
        pick,
        flops=4 * tiles * (hi - lo) * JB * TILE * CL * NB,
    )


def gathered(slots):
    return jnp.concatenate([fold(s) for s in slots], axis=0)


def rolled(slots):
    return [*slots[LEAD:], *slots[:LEAD]]


def y_send(slots, kt_other, tiles):
    def body(*refs):
        slot_refs, (ko, send) = refs[: len(slots)], refs[len(slots) :]
        stack = gathered([s[...] for s in slot_refs])
        send[...] = dot(ko[...], stack).reshape(LB, TILE, NB).astype(BF)

    return call(
        body,
        (tiles,),
        [pl.BlockSpec((s.shape[0], TILE, NB), lambda t: (0, t, 0)) for s in slots]
        + [whole((CL, RW))],
        pl.BlockSpec((LB, TILE, NB), lambda t: (0, t, 0)),
        jax.ShapeDtypeStruct((LB, tiles * TILE, NB), BF),
        (*slots, kt_other),
        flops=2 * tiles * RW * CL * NB,
    )


def y_keep(slots, kt_mine, pick, first, tiles):
    def body(_, *refs):
        slot_refs, (km, kept) = refs[: len(slots)], refs[len(slots) :]
        stack = gathered([s[...] for s in slot_refs])
        kept[0] = dot(km[...], stack).reshape(LB, TILE, NB).astype(BF)

    return call(
        body,
        (tiles,),
        [pl.BlockSpec((s.shape[0], TILE, NB), lambda t, s: (0, t, 0)) for s in slots]
        + [whole((CL, RW))],
        pl.BlockSpec((1, LB, TILE, NB), lambda t, s: (s[0], 0, first + t, 0)),
        jax.ShapeDtypeStruct((2, LB, MB, NB), BF),
        (*slots, kt_mine),
        pick,
        flops=2 * tiles * RW * CL * NB,
    )


def z_expand(slots, kt_mine, out, pick, first, tiles):
    def body(_, *refs):
        slot_refs, km, kept = refs[:NZ], refs[NZ], refs[NZ + 2]
        wide = dot(
            km[...], beside(lambda spot: gathered([s[0, :, spot] for s in slot_refs]), tiles)
        )
        for t in range(tiles):
            part = wide[:, t * NB : (t + 1) * NB].reshape(LB, TILE, NB)
            kept[0, :, t * TILE : (t + 1) * TILE] = part.astype(BF)

    return call(
        body,
        (2,),
        [pl.BlockSpec((1, JB, tiles * TILE, NB), lambda o, s: (o, 0, 0, 0))] * NZ
        + [whole((CL, RW)), pl.BlockSpec(memory_space=pl.ANY)],
        pl.BlockSpec(
            tuple(pl.Element(n) for n in (1, LB, tiles * TILE, NB)),
            lambda o, s: (s[o], 0, first * TILE, 0),
        ),
        jax.ShapeDtypeStruct((2, LB, MB, NB), BF),
        (*slots, kt_mine, out),
        pick,
        {NZ + 2: 0},
        flops=4 * tiles * RW * CL * NB,
    )


def put(got, out):
    def body(src, _, dst, sem):
        there = 1 - lax.axis_index("ylo")
        copies = [
            pltpu.make_async_copy(
                src.at[pl.ds(i * CUT, CUT)],
                dst.at[there, pl.ds(i * CUT, CUT), pl.ds(0, YM), :],
                sem.at[i],
            )
            for i in range(CUTS)
        ]
        for copy in copies:
            copy.start()
        for copy in copies:
            copy.wait()

    return pl.pallas_call(
        body,
        in_specs=[
            pl.BlockSpec(memory_space=pl.ANY),
            pl.BlockSpec(memory_space=pltpu.HBM),
        ],
        out_specs=pl.BlockSpec(memory_space=pltpu.HBM),
        out_shape=jax.ShapeDtypeStruct((2, LB, MB, NB), BF),
        scratch_shapes=[pltpu.SemaphoreType.DMA((CUTS,))],
        input_output_aliases={1: 0},
        name="put",
        cost_estimate=pl.CostEstimate(flops=0, bytes_accessed=4 * LB * YM * NB, transcendentals=0),
        compiler_params=pltpu.CompilerParams(vmem_limit_bytes=24 * 1024 * 1024),
    )(got, out)


def to_virtual(summed, vt_halves):
    def body(s, v, out):
        flat = s[...].astype(F32).reshape(JB * MB, NB).astype(BF)
        wide = lax.dot_general(flat, v[0], (((1,), (1,)), ((), ())), preferred_element_type=F32)
        out[...] = wide.reshape(JB, MB, HALF).astype(BF)

    return call(
        body,
        (2,),
        [whole((JB, MB, NB)), pl.BlockSpec((1, HALF, NB), lambda h: (h, 0, 0))],
        pl.BlockSpec((JB, MB, HALF), lambda h: (h, 0, 0)),
        jax.ShapeDtypeStruct((NROW, MB, HALF), BF),
        (summed, vt_halves),
        flops=2 * JB * MB * NB * NV,
    )


def divide(second, coef, coef_t, column, row):
    def body(x, v, vt, c, r, out):
        third = dot(vt[...], x[...])
        amplitude = (third / (c[...] + r[...])).astype(BF)
        out[...] = dot(v[...], amplitude).astype(BF)

    return call(
        body,
        (1,),
        [whole((NB, HALF)), whole((NB, NV)), whole((NV, NB)), whole((NV, 1)), whole((1, HALF))],
        whole((NB, HALF)),
        jax.ShapeDtypeStruct((NB, HALF), BF),
        (second, coef, coef_t, column, row),
        flops=4 * NB * HALF * NV,
    )


def to_basis(back, vt_halves, sizes):
    def body(x, v, *outs):
        flat = [
            x[h * JB : (h + 1) * JB].astype(F32).reshape(JB * MB, HALF).astype(BF) for h in range(2)
        ]
        wide = (dot(flat[0], v[0]) + dot(flat[1], v[1])).reshape(JB, MB, NB)
        lo = 0
        for out, size in zip(outs, sizes):
            out[...] = wide[:, lo : lo + size].astype(BF)
            lo += size

    return call(
        body,
        (1,),
        [whole((NROW, MB, HALF)), whole((2, HALF, NB))],
        [whole((JB, size, NB)) for size in sizes],
        [jax.ShapeDtypeStruct((JB, size, NB), BF) for size in sizes],
        (back, vt_halves),
        flops=2 * JB * MB * NB * NV,
    )


def add(*terms):
    total = terms[0].astype(F32)
    for term in terms[1:]:
        total = total + term.astype(F32)
    return total.astype(BF)


def move(x, step):
    return lax.ppermute(x, "z", [(i, (i + step) % NZ) for i in range(NZ)])


def swap(x):
    return lax.ppermute(x, "ylo", SWAP)


def unrolled(parts):
    return [*parts[NZ - LEAD :], *parts[: NZ - LEAD]]


def chain_sum(parts):
    up, down = parts[3], parts[FAR]
    for n in range(1, FAR + 1):
        if n < FAR:
            up = move(up, 1)
            up = add(up, parts[3 - n]) if n < 3 else up
        down = move(down, -1)
        down = add(down, parts[FAR + n]) if n < FAR else down
    return add(parts[0], up, down)


def tree_sum(parts):
    up = move(parts[3], 1)
    down = move(parts[5], -1)
    far = move(parts[FAR], 2)
    up = add(up, parts[2], far)
    down = add(down, parts[6])
    up = add(move(up, 1), parts[1])
    down = add(move(down, -1), parts[7])
    return add(parts[0], move(up, 1), move(down, -1))


def chain_gather(own):
    slots = [own] + [None] * (NZ - 1)
    up = down = own
    for n in range(1, FAR + 1):
        if n < FAR:
            up = slots[NZ - n] = move(up, 1)
        down = slots[n] = move(down, -1)
    return rolled(slots)


def tree_gather(own):
    up1 = move(own, 1)
    down1 = move(own, -1)
    up2 = move(up1, 1)
    down2 = move(down1, -1)
    up3 = move(up2, 1)
    down3 = move(down2, -1)
    high = move(up2[:JH], 2)
    low = move(down2[JH:], -2)
    return [down3, high, low, up3, up2, up1, own, down1, down2]


def run(slab, coef_virtual, coef_occupied, occ_level, virt_level, orbital_index):
    zi = lax.axis_index("z")
    yi = lax.axis_index("ylo")
    ri = lax.axis_index("row")
    slab = pltpu.with_memory_space_constraint(slab, pltpu.HBM)
    pick = jnp.stack([yi, 1 - yi]).astype(jnp.int32)
    eo = occ_level.astype(F32) / 64.0
    ev = virt_level.astype(F32) / 64.0
    occs = jnp.arange(NO, dtype=jnp.int32)
    chosen = jnp.sum(jnp.where(jnp.arange(2) == yi, orbital_index, 0))
    energy_i = jnp.sum(jnp.where(occs == chosen, eo, 0.0))
    energy_j = jnp.sum(jnp.where(occs == zi * JB + ri % JB, eo, 0.0))
    row = (jnp.where(ri // JB == 0, ev[:HALF], ev[HALF:]) - energy_i - energy_j)[None, :]
    column = ev[:, None]
    coef_t = coef_virtual.T
    vt_halves = coef_t.reshape(2, HALF, NB)

    raised, coef_o = lax.optimization_barrier((lift(slab), coef_occupied.T))
    swapped = swap(raised)
    k_mine = spread(coef_o, zi * 2 * LB + yi * LB, zi)
    k_other = spread(coef_o, zi * 2 * LB + (1 - yi) * LB, zi)
    head = z_parts(slab, k_mine, pick, YT, ZT, 0, 2)
    tail = z_parts(slab, k_mine, pick, YT, ZT, 2, NZ)
    both = chain_sum(unrolled([*head, *tail]))
    last = add(both[0], swap(both[1]))
    head = y_parts(slab, swapped, k_mine, k_other, pick, 0, YT, 0, 3)
    tail = y_parts(slab, swapped, k_mine, k_other, pick, 0, YT, 3, NZ)
    lead = tree_sum(unrolled([*head, *tail]))
    summed = jnp.concatenate([lead, last], axis=1)

    first = to_virtual(summed, vt_halves)
    first, coef_late = lax.optimization_barrier((first, coef_virtual))
    second = lax.all_to_all(first, "row", 0, 0, tiled=True).reshape(NB, HALF)
    back_one = divide(second, coef_late, coef_t, column, row)
    back = lax.all_to_all(back_one.reshape(NROW, MB, HALF), "row", 0, 0, tiled=True)
    wide_y, wide_z = to_basis(back, vt_halves, (YM, ZM))

    kt_mine, kt_other = k_mine.T, k_other.T
    slots = tree_gather(wide_y)
    got = swap(y_send(slots, kt_other, YT))
    out = y_keep(slots, kt_mine, pick, 0, YT)
    both = jnp.stack([wide_z, swap(wide_z)])
    out = z_expand(chain_gather(both), kt_mine, out, pick, YT, ZT)
    return put(got, out)


def solution(mesh):
    fine = Mesh(mesh.devices.reshape(NROW, NZ, 2), ("row", "z", "ylo"))
    slab = P(None, ("z", "ylo"), "row", None)
    return jax.shard_map(
        run, mesh=fine, in_specs=(slab, P(), P(), P(), P(), P()), out_specs=slab, check_vma=False
    )
```
